512 devices in a mesh: pix: 128 (over z, x_lo, y), batch: 4 (over x_hi, core).
Axes of the slice: x: 4 (x_hi: 2, x_lo: 2; x = x_hi * 2 + x_lo), y: 4, z: 16, core: 2. Of those that a mesh axis runs over, the one named last changes fastest.
Arguments:
- fine_tokens: bfloat16 [524288, 512], P(('batch', 'pix')), parts along dimension 0, may hold values from -8 to 8
- parent_tokens: bfloat16 [131072, 512], P(('batch', 'pix')), parts along dimension 0, may hold values from -8 to 8
- shift_table: int32 [131072], P('pix'), may hold values from 0 to 131071, as said below
- parent_slot: int32 [32768], P('pix'), may hold values from 0 to 255, as said below
- fine_gain: float32 [512], replicated, may hold values from 0.1 to 1.9
- parent_gain: float32 [512], replicated, may hold values from 0.1 to 1.9
- w_qkv: bfloat16 [512, 1536], replicated, may hold values from -2 to 2
- w_parent: bfloat16 [512, 1024], replicated, may hold values from -2 to 2
- w_out: bfloat16 [1024, 512], replicated, may hold values from -0.1875 to 0.1875
Outputs:
- mixed: bfloat16 [524288, 512], P(('batch', 'pix')), parts along dimension 0
The draws below stay inside these ranges and needn't reach their ends.
There are 4 independent parts, one for each index of `batch`. The reference program is written for one: setup_inputs(seed, part) draws one part's arguments, and reference() takes and returns one part's arrays. A program takes and returns all parts, laid end to end along the dimension named above; an argument that names none is the same for every part. Nothing has to cross between parts.
Inputs may be any that keep to these rules, and one draw needn't show every extreme that they name: Every entry shift_table[p] equals (p + o) mod 131072 with -128 <= o <= 128; on every device one entry has o = 128 and one o = -128. Over the stored rows of one owner j, parent_slot takes every value 0 to 255 once.
All inputs are finite; a program needn't handle non-finite values.
Results may differ from the reference program's by a relative error of at most 0.0018.
The reference program's roundings to bfloat16 on the way count: a program that leaves them out, or rounds other values in their place, can miss the bound.
Values may be sent and summed in bfloat16 or wider, within the bound.
A program may use at most 64 MiB of HBM per device.

```python
import jax
import jax.numpy as jnp
from jax import lax

D = 512
HEADS = 16
HD = 32
WIN = 256
HALO = 128
PWIN = 64
PIX_DEV = 1024
PAR_DEV = 256
NPIX = 131072
NPAR = 32768
N_PIX = 128


def draw_shift_table(key, part):
    everything = jnp.arange(NPIX, dtype=jnp.int32)
    offsets = jax.random.randint(key, (NPIX,), -HALO, HALO + 1, dtype=jnp.int32)
    within = everything % PIX_DEV
    offsets = jnp.where(within == 0, HALO, offsets)
    offsets = jnp.where(within == 1, -HALO, offsets)
    offsets = jnp.where(within == 2, -3, offsets)
    offsets = jnp.where(within == 3, -3, offsets)
    return jnp.mod(everything + offsets, NPIX).astype(jnp.int32)


def draw_parent_slot(key, part):
    owners = NPAR // PAR_DEV
    block_rows = PAR_DEV // owners
    subkeys = jax.random.split(jax.random.fold_in(key, 7), owners)
    orders = jax.vmap(lambda single: jax.random.permutation(single, PAR_DEV))(subkeys)
    table = orders.reshape(owners, owners, block_rows)
    return jnp.transpose(table, (1, 0, 2)).reshape(NPAR).astype(jnp.int32)


def draw_fine_tokens(key, part):
    sub = jax.random.fold_in(key, 31)
    values = jnp.clip(jax.random.normal(sub, (NPIX, D), jnp.float32), -6.0, 6.0)
    return values.astype(jnp.bfloat16)


def draw_parent_tokens(key, part):
    sub = jax.random.fold_in(key, 32)
    values = jnp.clip(jax.random.normal(sub, (NPAR, D), jnp.float32), -6.0, 6.0)
    return values.astype(jnp.bfloat16)


def draw_fine_gain(key, part):
    sub = jax.random.fold_in(key, 21)
    values = 1.0 + 0.18 * jnp.clip(jax.random.normal(sub, (D,), jnp.float32), -5.0, 5.0)
    return values.astype(jnp.float32)


def draw_parent_gain(key, part):
    sub = jax.random.fold_in(key, 22)
    values = 1.0 + 0.18 * jnp.clip(jax.random.normal(sub, (D,), jnp.float32), -5.0, 5.0)
    return values.astype(jnp.float32)


def draw_w_qkv(key, part):
    sub = jax.random.fold_in(key, 11)
    scale = D ** (-0.5)
    values = jnp.clip(jax.random.normal(sub, (D, 3 * D), jnp.float32), -4.0, 4.0) * scale
    return values.astype(jnp.bfloat16)


def draw_w_parent(key, part):
    sub = jax.random.fold_in(key, 12)
    scale = D ** (-0.5)
    values = jnp.clip(jax.random.normal(sub, (D, 2 * D), jnp.float32), -4.0, 4.0) * scale
    return values.astype(jnp.bfloat16)


def scatter_about(stream_key, shape, spread, most, held_as=jnp.bfloat16):
    return jnp.clip(spread * jax.random.normal(stream_key, shape, jnp.float32), -most, most).astype(held_as)


def setup_inputs(seed: int = 0, part: int = 0) -> dict:
    key_list = jax.random.split(jax.random.key(seed), 10)
    part_splits = jax.random.split(jax.random.fold_in(key_list[9], part), 10)
    return {
        "fine_tokens": draw_fine_tokens(jax.random.fold_in(jax.random.fold_in(key_list[9], part), 71), part),
        "parent_tokens": draw_parent_tokens(jax.random.fold_in(jax.random.fold_in(key_list[9], part), 71), part),
        "shift_table": draw_shift_table(jax.random.fold_in(key_list[9], 71), part),
        "parent_slot": draw_parent_slot(jax.random.fold_in(key_list[9], 71), part),
        "fine_gain": draw_fine_gain(jax.random.fold_in(key_list[9], 71), part),
        "parent_gain": draw_parent_gain(jax.random.fold_in(key_list[9], 71), part),
        "w_qkv": draw_w_qkv(jax.random.fold_in(key_list[9], 71), part),
        "w_parent": draw_w_parent(jax.random.fold_in(key_list[9], 71), part),
        "w_out": scatter_about(key_list[8], (2 * D, D), (2 * D) ** -0.5, 0.1875),
    }


def rms_rows(matrix, gain):
    values = matrix.astype(jnp.float32)
    factor = lax.rsqrt(lax.optimization_barrier(jnp.mean(values * values, axis=-1, keepdims=True)) + 1e-06)
    return (values * factor * gain.astype(jnp.float32)).astype(jnp.bfloat16)

def attend(queries, key_heads, value_heads):
    scores = jnp.einsum('wrhe,wshe->whrs', queries.astype(jnp.float32), key_heads.astype(jnp.float32))
    scores = scores / jnp.sqrt(jnp.float32(HD))
    highest = lax.optimization_barrier(jnp.max(scores, axis=-1, keepdims=True))
    powers = jnp.exp(scores - highest)
    weights = (powers / lax.optimization_barrier(jnp.sum(powers, axis=-1, keepdims=True))).astype(jnp.bfloat16)
    result = jnp.einsum('whrs,wshe->wrhe', weights.astype(jnp.float32), value_heads.astype(jnp.float32))
    return result.astype(jnp.bfloat16)

def reference(fine_tokens, parent_tokens, shift_table, parent_slot, fine_gain, parent_gain, w_qkv, w_parent, w_out):
    block_rows = PAR_DEV * PAR_DEV // NPAR
    stored = jnp.arange(NPAR, dtype=jnp.int32)
    owners = stored % PAR_DEV // block_rows
    target = (owners * PAR_DEV + parent_slot).astype(jnp.int32)
    parents = jnp.zeros_like(parent_tokens).at[target].set(parent_tokens)
    normed = rms_rows(fine_tokens, fine_gain)
    qkv = jnp.dot(normed, w_qkv, preferred_element_type=jnp.float32).astype(jnp.bfloat16)
    parent_kv = jnp.dot(rms_rows(parents, parent_gain), w_parent, preferred_element_type=jnp.float32).astype(jnp.bfloat16)
    window_kv = jnp.take(qkv[:, D:], shift_table, axis=0)
    per_dev = PIX_DEV // WIN
    queries = qkv[:, :D].reshape(N_PIX, per_dev, WIN, HEADS, HD)
    self_keys = window_kv[:, :D].reshape(N_PIX, per_dev, WIN, HEADS, HD)
    self_values = window_kv[:, D:].reshape(N_PIX, per_dev, WIN, HEADS, HD)
    cross_keys = parent_kv[:, :D].reshape(N_PIX, per_dev, PWIN, HEADS, HD)
    cross_values = parent_kv[:, D:].reshape(N_PIX, per_dev, PWIN, HEADS, HD)

    def one_group(pieces):
        group_q, group_k, group_v, group_pk, group_pv = pieces
        self_out = attend(group_q, group_k, group_v).reshape(PIX_DEV, D)
        cross_out = attend(group_q, group_pk, group_pv).reshape(PIX_DEV, D)
        return jnp.concatenate([self_out, cross_out], axis=1)
    joined = lax.map(one_group, (queries, self_keys, self_values, cross_keys, cross_values))
    joined = joined.reshape(NPIX, 2 * D)
    branch = jnp.dot(joined, w_out, preferred_element_type=jnp.float32)
    return (fine_tokens.astype(jnp.float32) + branch).astype(jnp.bfloat16)
```

```python
import functools

import jax
import jax.numpy as jnp
from jax import lax
from jax.experimental import pallas as pl
from jax.experimental.pallas import tpu as pltpu
from jax.sharding import PartitionSpec as P

HEADS = 16
WIN = 256
HALO = 128
PWIN = 64
ZN = 16
XYN = 8
NEAR = (0, 1, 2, 3, 4, 13, 14, 15)
FAR = (8, 7, 9, 6, 10, 5, 11, 12)
MESH = pl.DeviceIdType.MESH
F32 = jnp.float32
BF16 = jnp.bfloat16
SCALE = 1.4426950408889634 / (32.0**0.5)

NN = (((1,), (0,)), ((), ()))
NT = (((1,), (1,)), ((), ()))
TN = (((0,), (0,)), ((), ()))


def dot(a, b, dims=NN):
    return lax.dot_general(a, b, dims, preferred_element_type=F32)


def rms_rows(rows, gain):
    values = rows.astype(F32)
    factor = lax.rsqrt(jnp.mean(values * values, axis=-1, keepdims=True) + 1e-06)
    return (values * factor * gain).astype(BF16)


def softmax_rows(scores):
    powers = jnp.exp2((scores - jnp.max(scores, axis=0, keepdims=True)) * SCALE)
    return (powers * (1.0 / jnp.sum(powers, axis=0, keepdims=True))).astype(BF16)


def kernel(
    fine, par, shift, pslot, fgain, pgain, wqkv, wpar, wout, out,
    xv, ext, halo, qv, kv, vt, ot, acc, relb, shv, fgv, pgv,
    wq, wp, wo, wvt, wpvt, zbuf, tbuf, fbuf, zslot, fslot, kpv, vpt, ov,
    in_sem, out_sem, own_sem, hs_sem, hr_sem, zs_sem, zr_sem, zss_sem, zsr_sem,
    ps_sem, pr_sem, pss_sem, psr_sem,
):
    me = lax.axis_index("pix")
    count = ZN * XYN
    z = me // XYN
    xy = me % XYN
    right = (me + 1) % count
    left = (me + count - 1) % count
    rows = xv.shape[0]
    features = xv.shape[1]
    windows = rows // WIN
    total = rows * count

    loads = [
        pltpu.make_async_copy(fine.at[pl.ds(WIN * i, WIN)], xv.at[pl.ds(WIN * i, WIN)], in_sem.at[i])
        for i in range(4)
    ]
    loads.append(pltpu.make_async_copy(fgain, fgv, in_sem.at[4]))
    loads.append(pltpu.make_async_copy(shift, shv, in_sem.at[5]))
    loads.append(pltpu.make_async_copy(wqkv, wq, in_sem.at[6]))
    loads.append(pltpu.make_async_copy(wpar, wp, in_sem.at[7]))
    loads.append(pltpu.make_async_copy(wout, wo, in_sem.at[8]))
    loads.append(pltpu.make_async_copy(pgain, pgv, in_sem.at[9]))

    barrier = pltpu.get_barrier_semaphore()
    peers = [((z + k) % ZN) * XYN + xy for k in range(1, ZN)]
    peers += [z * XYN + (xy + m) % XYN for m in range(1, XYN)]
    peers += [left, right]
    for peer in peers:
        pl.semaphore_signal(barrier, inc=1, device_id={"pix": peer}, device_id_type=MESH)
    for load in loads:
        load.start()

    loads[4].wait()
    loads[5].wait()
    place = lax.broadcasted_iota(jnp.int32, (8, 128), 0) * 128 + lax.broadcasted_iota(
        jnp.int32, (8, 128), 1
    )
    away = shv[...] - (place + me * rows)
    away = jnp.where(away > total // 2, away - total, away)
    away = jnp.where(away < -(total // 2), away + total, away)
    rel = ((place % WIN) + away + HALO).astype(F32)
    for i in range(8):
        relb[128 * i : 128 * (i + 1), :] = jnp.transpose(
            jnp.broadcast_to(rel[i : i + 1, :], (128, 128))
        )
    gain = fgv[...]
    for i in range(4):
        loads[i].wait()

        def norm_step(s, carry):
            at = pl.multiple_of(WIN * i + 64 * s, 64)
            ext[pl.ds(pl.multiple_of(at + HALO, 64), 64), :] = rms_rows(xv[pl.ds(at, 64), :], gain)
            return carry

        lax.fori_loop(0, WIN // 64, norm_step, 0)
    loads[6].wait()
    wvt[...] = jnp.transpose(wq[:, 2 * features :])

    pl.semaphore_wait(barrier, len(peers))

    def remote(src, dst, send, recv, peer):
        return pltpu.make_async_remote_copy(
            src_ref=src, dst_ref=dst, send_sem=send, recv_sem=recv,
            device_id={"pix": peer}, device_id_type=MESH,
        )

    to_left = remote(fine.at[pl.ds(0, HALO)], halo.at[1], hs_sem.at[0], hr_sem.at[0], left)
    to_right = remote(
        fine.at[pl.ds(rows - HALO, HALO)], halo.at[0], hs_sem.at[1], hr_sem.at[1], right
    )
    to_left.start()
    to_right.start()

    own = [
        pltpu.make_async_copy(
            par.at[pl.ds(pl.multiple_of(16 * z, 16), 16)], zbuf.at[0, pl.ds(0, 16)], own_sem.at[0]
        ),
        pltpu.make_async_copy(pslot.at[z // 8], zslot.at[0, 0], own_sem.at[1]),
    ]
    for copy in own:
        copy.start()
    along_z = {}
    for half, ks in enumerate((NEAR, FAR)):
        for kk, k in enumerate(ks):
            if k == 0:
                continue
            there = (z + k) % ZN
            peer = there * XYN + xy
            data = remote(
                par.at[pl.ds(pl.multiple_of(16 * there, 16), 16)],
                zbuf.at[half, pl.ds(16 * kk, 16)],
                zs_sem.at[k], zr_sem.at[k], peer,
            )
            slot = remote(
                pslot.at[there // 8], zslot.at[half, kk], zss_sem.at[k], zsr_sem.at[k], peer
            )
            along_z[k] = (data, slot)
    for k in FAR + NEAR[1:]:
        along_z[k][0].start()
        along_z[k][1].start()

    lanes128 = lax.broadcasted_iota(jnp.int32, (1, 128), 1)
    lane_rows = lax.broadcasted_iota(jnp.int32, (WIN, 128), 1).astype(F32)
    head_masks = [(lanes128 // 32 == t).astype(F32).astype(BF16) for t in range(4)]

    def window(i, carry):
        w = (i + 1) % windows
        base = pl.multiple_of(w * WIN, WIN)
        own_rows = ext[pl.ds(pl.multiple_of(base + HALO, HALO), WIN), :]
        qv[pl.ds(base, WIN), :] = dot(own_rows, wq[:, :features]).astype(BF16)
        where = relb[pl.ds(base, WIN), :]
        picks = jnp.concatenate(
            [(where == lane_rows + 128.0 * c).astype(F32).astype(BF16) for c in range(4)], axis=1
        )
        gathered = dot(picks, ext[pl.ds(base, 2 * WIN), :]).astype(BF16)
        kv[...] = dot(gathered, wq[:, features : 2 * features]).astype(BF16)
        vt[...] = dot(wvt[...], gathered, NT).astype(BF16)

        def group(g, carry):
            at = pl.multiple_of(g * 128, 128)
            keys = kv[:, pl.ds(at, 128)]
            queries = qv[pl.ds(base, WIN), pl.ds(at, 128)]
            for t in range(4):
                weights = softmax_rows(dot(keys * head_masks[t], queries, NT))
                there = pl.multiple_of(at + 32 * t, 32)
                ot[pl.ds(there, 32), :] = dot(vt[pl.ds(there, 32), :], weights).astype(BF16)
            return carry

        lax.fori_loop(0, HEADS // 4, group, 0)
        acc[pl.ds(base, WIN), :] = dot(jnp.transpose(ot[...]), wo[:features, :])
        return carry

    loads[8].wait()
    lax.fori_loop(0, 2, window, 0)

    to_left.wait_recv()
    to_right.wait_recv()
    ext[:HALO, :] = rms_rows(halo[0], gain)
    ext[HALO + rows :, :] = rms_rows(halo[1], gain)
    lax.fori_loop(2, 4, window, 0)

    loads[7].wait()
    loads[9].wait()
    wpvt[...] = jnp.transpose(wp[:, features:])

    a = lax.broadcasted_iota(jnp.int32, (128, 128), 0)
    b = lax.broadcasted_iota(jnp.int32, (128, 128), 1)
    order = (b == (a % 8) * 16 + (a // 16) * 2 + (a // 8) % 2).astype(F32).astype(BF16)
    plane = []
    for half, ks in ((1, FAR), (0, NEAR)):
        for k in ks:
            for copy in own if k == 0 else along_z[k]:
                if k == 0:
                    copy.wait()
                else:
                    copy.wait_recv()
        tbuf[half] = dot(order, zbuf[half]).astype(BF16)
        for m in range(1, XYN):
            there = (xy + m) % XYN
            peer = z * XYN + there
            data = remote(
                tbuf.at[half, pl.ds(pl.multiple_of(16 * there, 16), 16)],
                fbuf.at[half, pl.ds(16 * m, 16)],
                ps_sem.at[half, m], pr_sem.at[half, m], peer,
            )
            slot = remote(
                zslot.at[half], fslot.at[half, m], pss_sem.at[half, m], psr_sem.at[half, m], peer
            )
            data.start()
            slot.start()
            plane += [data, slot]
        fbuf[half, 0:16, :] = tbuf[half, pl.ds(pl.multiple_of(16 * xy, 16), 16), :]
        fslot[half, 0] = zslot[half]

    for copy in plane:
        copy.wait_recv()
    table = fslot[...].reshape(128, 128).astype(F32).astype(BF16)
    first = 16 * (z % 8) + 2 * xy
    wanted = lax.broadcasted_iota(jnp.int32, (8, 128), 0) + first
    select = (lax.broadcasted_iota(jnp.int32, (8, 128), 1) == wanted).astype(F32).astype(BF16)
    slots = dot(select, table, NT).astype(BF16)
    ai = lax.broadcasted_iota(jnp.int32, (128, 256), 0)
    bi = lax.broadcasted_iota(jnp.int32, (128, 256), 1)
    same = (bi // 16 == ai // 8) & (bi % 8 == ai % 8)
    spread = [
        dot(slots, (same & ((bi // 8) % 2 == t)).astype(F32).astype(BF16))[t : t + 1, :]
        for t in range(2)
    ]
    position = spread[0] + spread[1]
    targets = lax.broadcasted_iota(jnp.int32, (256, 256), 0).astype(F32)
    placing = (targets == position).astype(F32).astype(BF16)
    parents = dot(placing, fbuf[...].reshape(256, features)).astype(BF16)
    pnormed = rms_rows(parents, pgv[...])
    kpv[...] = dot(pnormed, wp[:, :features]).astype(BF16)
    vpt[...] = dot(wpvt[...], pnormed, NT).astype(BF16)

    blank = jnp.zeros((PWIN, WIN), BF16)
    stores = []
    for w in range(windows):
        pair = 128 * (w // 2)

        def group(g, carry):
            at = pl.multiple_of(g * 128, 128)
            keys = kpv[PWIN * w : PWIN * (w + 1), pl.ds(at, 128)]
            queries = qv[WIN * w : WIN * (w + 1), pl.ds(at, 128)]
            for t in range(4):
                weights = softmax_rows(dot(keys * head_masks[t], queries, NT))
                parts = [weights, blank] if w % 2 == 0 else [blank, weights]
                there = pl.multiple_of(at + 32 * t, 32)
                ot[pl.ds(there, 32), :] = dot(
                    vpt[pl.ds(there, 32), pair : pair + 128], jnp.concatenate(parts, axis=0)
                ).astype(BF16)
            return carry

        lax.fori_loop(0, HEADS // 4, group, 0)
        here = slice(WIN * w, WIN * (w + 1))
        branch = acc[here, :] + dot(jnp.transpose(ot[...]), wo[features:, :])
        ov[here, :] = (xv[here, :].astype(F32) + branch).astype(BF16)
        store = pltpu.make_async_copy(
            ov.at[pl.ds(WIN * w, WIN)], out.at[pl.ds(WIN * w, WIN)], out_sem.at[w]
        )
        store.start()
        stores.append(store)

    to_left.wait_send()
    to_right.wait_send()
    for k in range(1, ZN):
        for copy in along_z[k]:
            copy.wait_send()
    for copy in plane:
        copy.wait_send()
    for store in stores:
        store.wait()


def on_device(
    fine_tokens,
    parent_tokens,
    shift_table,
    parent_slot,
    fine_gain,
    parent_gain,
    w_qkv,
    w_parent,
    w_out,
):
    rows, features = fine_tokens.shape
    dma = pltpu.SemaphoreType.DMA
    vmem = pltpu.VMEM
    return pl.pallas_call(
        kernel,
        out_shape=jax.ShapeDtypeStruct((rows, features), BF16),
        in_specs=[pl.BlockSpec(memory_space=pl.ANY)] * 9,
        out_specs=pl.BlockSpec(memory_space=pl.ANY),
        scratch_shapes=[
            vmem((rows, features), BF16),
            vmem((rows + 2 * HALO, features), BF16),
            vmem((2, HALO, features), BF16),
            vmem((rows, features), BF16),
            vmem((WIN, features), BF16),
            vmem((features, WIN), BF16),
            vmem((features, WIN), BF16),
            vmem((rows, features), F32),
            vmem((rows, 128), F32),
            vmem((8, 128), jnp.int32),
            vmem((1, features), F32),
            vmem((1, features), F32),
            vmem((features, 3 * features), BF16),
            vmem((features, 2 * features), BF16),
            vmem((2 * features, features), BF16),
            vmem((features, features), BF16),
            vmem((features, features), BF16),
            vmem((2, 128, features), BF16),
            vmem((2, 128, features), BF16),
            vmem((2, 128, features), BF16),
            vmem((2, 8, 1, 128), jnp.int32),
            vmem((2, 8, 8, 1, 128), jnp.int32),
            vmem((256, features), BF16),
            vmem((features, 256), BF16),
            vmem((rows, features), BF16),
            dma((10,)),
            dma((4,)),
            dma((2,)),
            dma((2,)),
            dma((2,)),
            dma((ZN,)),
            dma((ZN,)),
            dma((ZN,)),
            dma((ZN,)),
            dma((2, XYN)),
            dma((2, XYN)),
            dma((2, XYN)),
            dma((2, XYN)),
        ],
        compiler_params=pltpu.CompilerParams(collective_id=0, has_side_effects=True),
    )(
        fine_tokens,
        parent_tokens,
        shift_table.reshape(8, 128),
        parent_slot.reshape(2, 1, 128),
        fine_gain.reshape(1, features),
        parent_gain.reshape(1, features),
        w_qkv,
        w_parent,
        w_out,
    )


def solution(mesh):
    return jax.shard_map(
        on_device,
        mesh=mesh,
        in_specs=(
            P(("batch", "pix"), None),
            P(("batch", "pix"), None),
            P("pix"),
            P("pix"),
            P(),
            P(),
            P(),
            P(),
            P(),
        ),
        out_specs=P(("batch", "pix"), None),
        check_vma=False,
    )
```

```python
import functools

import jax
import jax.numpy as jnp
from jax import lax
from jax.experimental import pallas as pl
from jax.experimental.pallas import tpu as pltpu
from jax.sharding import PartitionSpec as P

HEADS = 16
WIN = 256
HALO = 128
PWIN = 64
ZN = 16
XYN = 8
NEAR = (0, 1, 2, 3, 4, 13, 14, 15)
FAR = (8, 7, 9, 6, 10, 5, 11, 12)
MESH = pl.DeviceIdType.MESH
F32 = jnp.float32
BF16 = jnp.bfloat16
SCALE = 1.4426950408889634 / (32.0**0.5)

NN = (((1,), (0,)), ((), ()))
NT = (((1,), (1,)), ((), ()))
TN = (((0,), (0,)), ((), ()))


def dot(a, b, dims=NN):
    return lax.dot_general(a, b, dims, preferred_element_type=F32)


def rms_rows(rows, gain):
    values = rows.astype(F32)
    factor = lax.rsqrt(jnp.mean(values * values, axis=-1, keepdims=True) + 1e-06)
    return (values * factor * gain).astype(BF16)


def softmax_rows(scores):
    powers = jnp.exp2((scores - jnp.max(scores, axis=0, keepdims=True)) * SCALE)
    return (powers * (1.0 / jnp.sum(powers, axis=0, keepdims=True))).astype(BF16)


def staged(units, depth, scores, values, sbufs, pbufs):
    slots = len(sbufs)
    for u in range(-2, units + 2):
        if 0 <= u + 2 < units:
            sbufs[(u + 2) % slots][...] = scores(u + 2)
        if 0 <= u < units:
            for c in range(2):
                cols = slice(128 * c, 128 * (c + 1))
                for first in range(0, WIN, depth):
                    block = slice(first, first + depth)
                    pbufs[u % slots][block, cols] = softmax_rows(sbufs[u % slots][block, cols])
        if 0 <= u - 2 < units:
            values(u - 2, pbufs[(u - 2) % slots][...])


def kernel(
    fine, par, shift, pslot, fgain, pgain, wqkv, wpar, wout, out,
    xv, ext, halo, qv, kv, vt, ot, acc, relb, shv, fgv, pgv,
    wq, wp, wo, wvt, wpvt, zbuf, tbuf, fbuf, zslot, fslot, kpv, vz, cot, ov,
    s0, s1, s2, s3, p0, p1, p2, p3,
    in_sem, out_sem, own_sem, hs_sem, hr_sem, zs_sem, zr_sem, zss_sem, zsr_sem,
    ps_sem, pr_sem, pss_sem, psr_sem,
):
    sbufs, pbufs = (s0, s1, s2, s3), (p0, p1, p2, p3)
    me = lax.axis_index("pix")
    count = ZN * XYN
    z = me // XYN
    xy = me % XYN
    right = (me + 1) % count
    left = (me + count - 1) % count
    rows = xv.shape[0]
    features = xv.shape[1]
    windows = rows // WIN
    total = rows * count

    loads = [
        pltpu.make_async_copy(fine.at[pl.ds(WIN * i, WIN)], xv.at[pl.ds(WIN * i, WIN)], in_sem.at[i])
        for i in range(4)
    ]
    loads.append(pltpu.make_async_copy(fgain, fgv, in_sem.at[4]))
    loads.append(pltpu.make_async_copy(shift, shv, in_sem.at[5]))
    loads.append(pltpu.make_async_copy(wqkv, wq, in_sem.at[6]))
    loads.append(pltpu.make_async_copy(wpar, wp, in_sem.at[7]))
    loads.append(pltpu.make_async_copy(wout, wo, in_sem.at[8]))
    loads.append(pltpu.make_async_copy(pgain, pgv, in_sem.at[9]))

    barrier = pltpu.get_barrier_semaphore()
    peers = [((z + k) % ZN) * XYN + xy for k in range(1, ZN)]
    peers += [z * XYN + (xy + m) % XYN for m in range(1, XYN)]
    peers += [left, right]
    for peer in peers:
        pl.semaphore_signal(barrier, inc=1, device_id={"pix": peer}, device_id_type=MESH)
    for load in loads:
        load.start()

    loads[4].wait()
    loads[5].wait()
    place = lax.broadcasted_iota(jnp.int32, (8, 128), 0) * 128 + lax.broadcasted_iota(
        jnp.int32, (8, 128), 1
    )
    away = shv[...] - (place + me * rows)
    away = jnp.where(away > total // 2, away - total, away)
    away = jnp.where(away < -(total // 2), away + total, away)
    rel = ((place % WIN) + away + HALO).astype(F32)
    for i in range(8):
        relb[128 * i : 128 * (i + 1), :] = jnp.transpose(
            jnp.broadcast_to(rel[i : i + 1, :], (128, 128))
        )
    gain = fgv[...]
    for i in range(4):
        loads[i].wait()

        def norm_step(s, carry):
            at = pl.multiple_of(WIN * i + 64 * s, 64)
            ext[pl.ds(pl.multiple_of(at + HALO, 64), 64), :] = rms_rows(xv[pl.ds(at, 64), :], gain)
            return carry

        lax.fori_loop(0, WIN // 64, norm_step, 0)
    loads[6].wait()
    wvt[...] = jnp.transpose(wq[:, 2 * features :])

    pl.semaphore_wait(barrier, len(peers))

    def remote(src, dst, send, recv, peer):
        return pltpu.make_async_remote_copy(
            src_ref=src, dst_ref=dst, send_sem=send, recv_sem=recv,
            device_id={"pix": peer}, device_id_type=MESH,
        )

    to_left = remote(fine.at[pl.ds(0, HALO)], halo.at[1], hs_sem.at[0], hr_sem.at[0], left)
    to_right = remote(
        fine.at[pl.ds(rows - HALO, HALO)], halo.at[0], hs_sem.at[1], hr_sem.at[1], right
    )
    to_left.start()
    to_right.start()

    own = [
        pltpu.make_async_copy(
            par.at[pl.ds(pl.multiple_of(16 * z, 16), 16)], zbuf.at[0, pl.ds(0, 16)], own_sem.at[0]
        ),
        pltpu.make_async_copy(pslot.at[z // 8], zslot.at[0, 0], own_sem.at[1]),
    ]
    for copy in own:
        copy.start()
    along_z = {}
    for half, ks in enumerate((NEAR, FAR)):
        for kk, k in enumerate(ks):
            if k == 0:
                continue
            there = (z + k) % ZN
            peer = there * XYN + xy
            data = remote(
                par.at[pl.ds(pl.multiple_of(16 * there, 16), 16)],
                zbuf.at[half, pl.ds(16 * kk, 16)],
                zs_sem.at[k], zr_sem.at[k], peer,
            )
            slot = remote(
                pslot.at[there // 8], zslot.at[half, kk], zss_sem.at[k], zsr_sem.at[k], peer
            )
            along_z[k] = (data, slot)
    for k in FAR + NEAR[1:]:
        along_z[k][0].start()
        along_z[k][1].start()

    lanes128 = lax.broadcasted_iota(jnp.int32, (1, 128), 1)
    lane_rows = lax.broadcasted_iota(jnp.int32, (WIN, 128), 1).astype(F32)
    head_masks = [(lanes128 // 32 == t).astype(F32).astype(BF16) for t in range(4)]

    def window(i, carry):
        w = (i + 1) % windows
        base = pl.multiple_of(w * WIN, WIN)
        own_rows = ext[pl.ds(pl.multiple_of(base + HALO, HALO), WIN), :]
        qv[pl.ds(base, WIN), :] = dot(own_rows, wq[:, :features]).astype(BF16)
        where = relb[pl.ds(base, WIN), :]
        picks = jnp.concatenate(
            [(where == lane_rows + 128.0 * c).astype(F32).astype(BF16) for c in range(4)], axis=1
        )
        gathered = dot(picks, ext[pl.ds(base, 2 * WIN), :]).astype(BF16)
        kv[...] = dot(gathered, wq[:, features : 2 * features]).astype(BF16)
        vt[...] = dot(wvt[...], gathered, NT).astype(BF16)

        def self_scores(h):
            at = 128 * (h // 4)
            keys = kv[:, at : at + 128] * head_masks[h % 4]
            return dot(keys, qv[pl.ds(base, WIN), at : at + 128], NT)

        def self_values(h, weights):
            ot[32 * h : 32 * h + 32, :] = dot(vt[32 * h : 32 * h + 32, :], weights).astype(BF16)

        staged(HEADS, WIN, self_scores, self_values, sbufs, pbufs)
        acc[pl.ds(base, WIN), :] = dot(jnp.transpose(ot[...]), wo[:features, :])
        return carry

    loads[8].wait()
    lax.fori_loop(0, 2, window, 0)

    to_left.wait_recv()
    to_right.wait_recv()
    ext[:HALO, :] = rms_rows(halo[0], gain)
    ext[HALO + rows :, :] = rms_rows(halo[1], gain)
    lax.fori_loop(2, 4, window, 0)

    loads[7].wait()
    loads[9].wait()
    wpvt[...] = jnp.transpose(wp[:, features:])

    a = lax.broadcasted_iota(jnp.int32, (128, 128), 0)
    b = lax.broadcasted_iota(jnp.int32, (128, 128), 1)
    order = (b == (a % 8) * 16 + (a // 16) * 2 + (a // 8) % 2).astype(F32).astype(BF16)
    plane = []
    for half, ks in ((1, FAR), (0, NEAR)):
        for k in ks:
            for copy in own if k == 0 else along_z[k]:
                if k == 0:
                    copy.wait()
                else:
                    copy.wait_recv()
        tbuf[half] = dot(order, zbuf[half]).astype(BF16)
        for m in range(1, XYN):
            there = (xy + m) % XYN
            peer = z * XYN + there
            data = remote(
                tbuf.at[half, pl.ds(pl.multiple_of(16 * there, 16), 16)],
                fbuf.at[half, pl.ds(16 * m, 16)],
                ps_sem.at[half, m], pr_sem.at[half, m], peer,
            )
            slot = remote(
                zslot.at[half], fslot.at[half, m], pss_sem.at[half, m], psr_sem.at[half, m], peer
            )
            data.start()
            slot.start()
            plane += [data, slot]
        fbuf[half, 0:16, :] = tbuf[half, pl.ds(pl.multiple_of(16 * xy, 16), 16), :]
        fslot[half, 0] = zslot[half]

    for copy in plane:
        copy.wait_recv()
    table = fslot[...].reshape(128, 128).astype(F32).astype(BF16)
    first = 16 * (z % 8) + 2 * xy
    wanted = lax.broadcasted_iota(jnp.int32, (8, 128), 0) + first
    select = (lax.broadcasted_iota(jnp.int32, (8, 128), 1) == wanted).astype(F32).astype(BF16)
    slots = dot(select, table, NT).astype(BF16)
    ai = lax.broadcasted_iota(jnp.int32, (128, 256), 0)
    bi = lax.broadcasted_iota(jnp.int32, (128, 256), 1)
    same = (bi // 16 == ai // 8) & (bi % 8 == ai % 8)
    spread = [
        dot(slots, (same & ((bi // 8) % 2 == t)).astype(F32).astype(BF16))[t : t + 1, :]
        for t in range(2)
    ]
    position = spread[0] + spread[1]
    targets = lax.broadcasted_iota(jnp.int32, (256, 256), 0).astype(F32)
    placing = (targets == position).astype(F32).astype(BF16)
    parents = dot(placing, fbuf[...].reshape(256, features)).astype(BF16)
    pnormed = rms_rows(parents, pgv[...])
    kpv[...] = dot(pnormed, wp[:, :features]).astype(BF16)
    block = (
        lax.broadcasted_iota(jnp.int32, (features, WIN), 0) // 32 % 4
        == lax.broadcasted_iota(jnp.int32, (features, WIN), 1) // PWIN
    ).astype(F32)
    for w in range(windows):
        part = pnormed[PWIN * w : PWIN * (w + 1), :]
        repeated = jnp.concatenate([part] * 4, axis=0)
        vz[w] = (dot(wpvt[...], repeated, NT) * block).astype(BF16)

    groups = HEADS // 4
    stores = []

    def cross_scores(u):
        w, at = u // groups, 128 * (u % groups)
        keys = kpv[PWIN * w : PWIN * (w + 1), at : at + 128]
        stacked = jnp.concatenate([keys * mask for mask in head_masks], axis=0)
        return dot(stacked, qv[WIN * w : WIN * (w + 1), at : at + 128], NT)

    def cross_values(u, weights):
        w, at = u // groups, 128 * (u % groups)
        cot[w, at : at + 128, :] = dot(vz[w, at : at + 128, :], weights).astype(BF16)
        if u % groups == groups - 1:
            here = slice(WIN * w, WIN * (w + 1))
            branch = acc[here, :] + dot(jnp.transpose(cot[w]), wo[features:, :])
            ov[here, :] = (xv[here, :].astype(F32) + branch).astype(BF16)
            store = pltpu.make_async_copy(
                ov.at[pl.ds(WIN * w, WIN)], out.at[pl.ds(WIN * w, WIN)], out_sem.at[w]
            )
            store.start()
            stores.append(store)

    staged(windows * groups, PWIN, cross_scores, cross_values, sbufs, pbufs)

    to_left.wait_send()
    to_right.wait_send()
    for k in range(1, ZN):
        for copy in along_z[k]:
            copy.wait_send()
    for copy in plane:
        copy.wait_send()
    for store in stores:
        store.wait()


def on_device(
    fine_tokens,
    parent_tokens,
    shift_table,
    parent_slot,
    fine_gain,
    parent_gain,
    w_qkv,
    w_parent,
    w_out,
):
    rows, features = fine_tokens.shape
    dma = pltpu.SemaphoreType.DMA
    vmem = pltpu.VMEM
    return pl.pallas_call(
        kernel,
        out_shape=jax.ShapeDtypeStruct((rows, features), BF16),
        in_specs=[pl.BlockSpec(memory_space=pl.ANY)] * 9,
        out_specs=pl.BlockSpec(memory_space=pl.ANY),
        scratch_shapes=[
            vmem((rows, features), BF16),
            vmem((rows + 2 * HALO, features), BF16),
            vmem((2, HALO, features), BF16),
            vmem((rows, features), BF16),
            vmem((WIN, features), BF16),
            vmem((features, WIN), BF16),
            vmem((features, WIN), BF16),
            vmem((rows, features), F32),
            vmem((rows, 128), F32),
            vmem((8, 128), jnp.int32),
            vmem((1, features), F32),
            vmem((1, features), F32),
            vmem((features, 3 * features), BF16),
            vmem((features, 2 * features), BF16),
            vmem((2 * features, features), BF16),
            vmem((features, features), BF16),
            vmem((features, features), BF16),
            vmem((2, 128, features), BF16),
            vmem((2, 128, features), BF16),
            vmem((2, 128, features), BF16),
            vmem((2, 8, 1, 128), jnp.int32),
            vmem((2, 8, 8, 1, 128), jnp.int32),
            vmem((256, features), BF16),
            vmem((4, features, WIN), BF16),
            vmem((4, features, WIN), BF16),
            vmem((rows, features), BF16),
            *[vmem((WIN, WIN), F32)] * 4,
            *[vmem((WIN, WIN), BF16)] * 4,
            dma((10,)),
            dma((4,)),
            dma((2,)),
            dma((2,)),
            dma((2,)),
            dma((ZN,)),
            dma((ZN,)),
            dma((ZN,)),
            dma((ZN,)),
            dma((2, XYN)),
            dma((2, XYN)),
            dma((2, XYN)),
            dma((2, XYN)),
        ],
        compiler_params=pltpu.CompilerParams(collective_id=0, has_side_effects=True),
    )(
        fine_tokens,
        parent_tokens,
        shift_table.reshape(8, 128),
        parent_slot.reshape(2, 1, 128),
        fine_gain.reshape(1, features),
        parent_gain.reshape(1, features),
        w_qkv,
        w_parent,
        w_out,
    )


def solution(mesh):
    return jax.shard_map(
        on_device,
        mesh=mesh,
        in_specs=(
            P(("batch", "pix"), None),
            P(("batch", "pix"), None),
            P("pix"),
            P("pix"),
            P(),
            P(),
            P(),
            P(),
            P(),
        ),
        out_specs=P(("batch", "pix"), None),
        check_vma=False,
    )
```

```python
import functools

import jax
import jax.numpy as jnp
from jax import lax
from jax.experimental import pallas as pl
from jax.experimental.pallas import tpu as pltpu
from jax.sharding import PartitionSpec as P

HEADS = 16
WIN = 256
HALO = 128
PWIN = 64
ZN = 16
XYN = 8
NEAR = (0, 1, 2, 3, 4, 13, 14, 15)
FAR = (8, 7, 9, 6, 10, 5, 11, 12)
MESH = pl.DeviceIdType.MESH
F32 = jnp.float32
BF16 = jnp.bfloat16
SCALE = 1.4426950408889634 / (32.0**0.5)

NN = (((1,), (0,)), ((), ()))
NT = (((1,), (1,)), ((), ()))
TN = (((0,), (0,)), ((), ()))


def dot(a, b, dims=NN):
    return lax.dot_general(a, b, dims, preferred_element_type=F32)


def rms_rows(rows, gain):
    values = rows.astype(F32)
    factor = lax.rsqrt(jnp.mean(values * values, axis=-1, keepdims=True) + 1e-06)
    return (values * factor * gain).astype(BF16)


def softmax_rows(scores):
    powers = jnp.exp2((scores - jnp.max(scores, axis=0, keepdims=True)) * SCALE)
    return (powers * (1.0 / jnp.sum(powers, axis=0, keepdims=True))).astype(BF16)


def staged(units, depth, scores, values, sbufs, pbufs):
    slots = len(sbufs)
    for u in range(-2, units + 2):
        if 0 <= u + 2 < units:
            sbufs[(u + 2) % slots][...] = scores(u + 2)
        if 0 <= u < units:
            for c in range(2):
                cols = slice(128 * c, 128 * (c + 1))
                for first in range(0, WIN, depth):
                    block = slice(first, first + depth)
                    pbufs[u % slots][block, cols] = softmax_rows(sbufs[u % slots][block, cols])
        if 0 <= u - 2 < units:
            values(u - 2, pbufs[(u - 2) % slots][...])


def kernel(
    fine, par, shift, pslot, fgain, pgain, wqkv, wpar, wout, out,
    xv, ext, halo, qv, kv, vt, ot, acc, relb, shv, fgv, pgv,
    wq, wp, wo, wvt, wpvt, zbuf, tbuf, fbuf, zslot, fslot, kpv, vz, cot, ov,
    s0, s1, s2, s3, p0, p1, p2, p3,
    in_sem, out_sem, own_sem, hs_sem, hr_sem, zs_sem, zr_sem, zss_sem, zsr_sem,
    ps_sem, pr_sem, pss_sem, psr_sem, far_sem,
):
    sbufs, pbufs = (s0, s1, s2, s3), (p0, p1, p2, p3)
    me = lax.axis_index("pix")
    count = ZN * XYN
    z = me // XYN
    xy = me % XYN
    right = (me + 1) % count
    left = (me + count - 1) % count
    rows = xv.shape[0]
    features = xv.shape[1]
    windows = rows // WIN
    total = rows * count

    loads = [
        pltpu.make_async_copy(fine.at[pl.ds(WIN * i, WIN)], xv.at[pl.ds(WIN * i, WIN)], in_sem.at[i])
        for i in range(4)
    ]
    loads.append(pltpu.make_async_copy(fgain, fgv, in_sem.at[4]))
    loads.append(pltpu.make_async_copy(shift, shv, in_sem.at[5]))
    loads.append(pltpu.make_async_copy(wqkv, wq, in_sem.at[6]))
    loads.append(pltpu.make_async_copy(wpar, wp, in_sem.at[7]))
    loads.append(pltpu.make_async_copy(wout, wo, in_sem.at[8]))
    loads.append(pltpu.make_async_copy(pgain, pgv, in_sem.at[9]))

    barrier = pltpu.get_barrier_semaphore()
    for load in loads:
        load.start()
    peers = [((z + k) % ZN) * XYN + xy for k in NEAR[1:] + (12,)]
    peers += [z * XYN + (xy + m) % XYN for m in range(1, XYN)]
    peers += [left, right]
    for peer in peers:
        pl.semaphore_signal(barrier, inc=1, device_id={"pix": peer}, device_id_type=MESH)

    loads[4].wait()
    loads[5].wait()
    place = lax.broadcasted_iota(jnp.int32, (8, 128), 0) * 128 + lax.broadcasted_iota(
        jnp.int32, (8, 128), 1
    )
    away = shv[...] - (place + me * rows)
    away = jnp.where(away > total // 2, away - total, away)
    away = jnp.where(away < -(total // 2), away + total, away)
    rel = ((place % WIN) + away + HALO).astype(F32)
    for i in range(8):
        relb[128 * i : 128 * (i + 1), :] = jnp.transpose(
            jnp.broadcast_to(rel[i : i + 1, :], (128, 128))
        )
    gain = fgv[...]
    for i in range(4):
        loads[i].wait()

        def norm_step(s, carry):
            at = pl.multiple_of(WIN * i + 64 * s, 64)
            ext[pl.ds(pl.multiple_of(at + HALO, 64), 64), :] = rms_rows(xv[pl.ds(at, 64), :], gain)
            return carry

        lax.fori_loop(0, WIN // 64, norm_step, 0)
    loads[6].wait()
    wvt[...] = jnp.transpose(wq[:, 2 * features :])

    pl.semaphore_wait(barrier, len(peers))
    for k in (4, 12):
        peer = ((z + k) % ZN) * XYN + xy
        pl.semaphore_signal(far_sem, inc=1, device_id={"pix": peer}, device_id_type=MESH)

    def remote(src, dst, send, recv, peer):
        return pltpu.make_async_remote_copy(
            src_ref=src, dst_ref=dst, send_sem=send, recv_sem=recv,
            device_id={"pix": peer}, device_id_type=MESH,
        )

    to_left = remote(fine.at[pl.ds(0, HALO)], halo.at[1], hs_sem.at[0], hr_sem.at[0], left)
    to_right = remote(
        fine.at[pl.ds(rows - HALO, HALO)], halo.at[0], hs_sem.at[1], hr_sem.at[1], right
    )

    own = [
        pltpu.make_async_copy(
            par.at[pl.ds(pl.multiple_of(16 * z, 16), 16)], zbuf.at[0, pl.ds(0, 16)], own_sem.at[0]
        ),
        pltpu.make_async_copy(pslot.at[z // 8], zslot.at[0, 0], own_sem.at[1]),
    ]
    for copy in own:
        copy.start()
    along_z = {}
    for half, ks in enumerate((NEAR, FAR)):
        for kk, k in enumerate(ks):
            if k == 0:
                continue
            there = (z + k) % ZN
            peer = there * XYN + xy
            data = remote(
                par.at[pl.ds(pl.multiple_of(16 * there, 16), 16)],
                zbuf.at[half, pl.ds(16 * kk, 16)],
                zs_sem.at[k], zr_sem.at[k], peer,
            )
            slot = remote(
                pslot.at[there // 8], zslot.at[half, kk], zss_sem.at[k], zsr_sem.at[k], peer
            )
            along_z[k] = (data, slot)
    for k in (4, 13, 3, 14, 2, 15, 1):
        along_z[k][1].start()
        along_z[k][0].start()
    to_left.start()
    to_right.start()

    lanes128 = lax.broadcasted_iota(jnp.int32, (1, 128), 1)
    lane_rows = lax.broadcasted_iota(jnp.int32, (WIN, 128), 1).astype(F32)
    head_masks = [(lanes128 // 32 == t).astype(F32).astype(BF16) for t in range(4)]

    def window(i, carry):
        w = (i + 1) % windows
        base = pl.multiple_of(w * WIN, WIN)
        own_rows = ext[pl.ds(pl.multiple_of(base + HALO, HALO), WIN), :]
        qv[pl.ds(base, WIN), :] = dot(own_rows, wq[:, :features]).astype(BF16)
        where = relb[pl.ds(base, WIN), :]
        picks = jnp.concatenate(
            [(where == lane_rows + 128.0 * c).astype(F32).astype(BF16) for c in range(4)], axis=1
        )
        gathered = dot(picks, ext[pl.ds(base, 2 * WIN), :]).astype(BF16)
        kv[...] = dot(gathered, wq[:, features : 2 * features]).astype(BF16)
        vt[...] = dot(wvt[...], gathered, NT).astype(BF16)

        def self_scores(h):
            at = 128 * (h // 4)
            keys = kv[:, at : at + 128] * head_masks[h % 4]
            return dot(keys, qv[pl.ds(base, WIN), at : at + 128], NT)

        def self_values(h, weights):
            ot[32 * h : 32 * h + 32, :] = dot(vt[32 * h : 32 * h + 32, :], weights).astype(BF16)

        staged(HEADS, WIN, self_scores, self_values, sbufs, pbufs)
        acc[pl.ds(base, WIN), :] = dot(jnp.transpose(ot[...]), wo[:features, :])
        return carry

    a = lax.broadcasted_iota(jnp.int32, (128, 128), 0)
    b = lax.broadcasted_iota(jnp.int32, (128, 128), 1)
    order = (b == (a % 8) * 16 + (a // 16) * 2 + (a // 8) % 2).astype(F32).astype(BF16)

    def second_phase(half, ks):
        for k in ks:
            if k == 0:
                own[1].wait()
            else:
                along_z[k][1].wait_recv()
        slots = [
            remote(
                zslot.at[half], fslot.at[half, m], pss_sem.at[half, m], psr_sem.at[half, m],
                z * XYN + (xy + m) % XYN,
            )
            for m in range(1, XYN)
        ]
        for copy in slots:
            copy.start()
        for k in ks:
            if k == 0:
                own[0].wait()
            else:
                along_z[k][0].wait_recv()
        tbuf[half] = dot(order, zbuf[half]).astype(BF16)
        fslot[half, 0] = zslot[half]
        fbuf[half, 0:16, :] = tbuf[half, pl.ds(pl.multiple_of(16 * xy, 16), 16), :]
        data = []
        for m in range(1, XYN):
            there = (xy + m) % XYN
            data.append(
                remote(
                    tbuf.at[half, pl.ds(pl.multiple_of(16 * there, 16), 16)],
                    fbuf.at[half, pl.ds(16 * m, 16)],
                    ps_sem.at[half, m], pr_sem.at[half, m], z * XYN + there,
                )
            )
        for copy in data:
            copy.start()
        return data, slots

    loads[8].wait()
    lax.fori_loop(0, 1, window, 0)
    pl.semaphore_wait(far_sem, 2)
    for k in FAR:
        along_z[k][1].start()
        along_z[k][0].start()
    lax.fori_loop(1, 2, window, 0)
    near_data, near_slots = second_phase(0, NEAR)

    to_left.wait_recv()
    to_right.wait_recv()
    ext[:HALO, :] = rms_rows(halo[0], gain)
    ext[HALO + rows :, :] = rms_rows(halo[1], gain)
    lax.fori_loop(2, 4, window, 0)

    loads[7].wait()
    loads[9].wait()
    wpvt[...] = jnp.transpose(wp[:, features:])
    far_data, far_slots = second_phase(1, FAR)
    plane = near_data + far_data + near_slots + far_slots

    for copy in near_slots + far_slots:
        copy.wait_recv()
    table = fslot[...].reshape(128, 128).astype(F32).astype(BF16)
    first = 16 * (z % 8) + 2 * xy
    wanted = lax.broadcasted_iota(jnp.int32, (8, 128), 0) + first
    select = (lax.broadcasted_iota(jnp.int32, (8, 128), 1) == wanted).astype(F32).astype(BF16)
    slots = dot(select, table, NT).astype(BF16)
    ai = lax.broadcasted_iota(jnp.int32, (128, 256), 0)
    bi = lax.broadcasted_iota(jnp.int32, (128, 256), 1)
    same = (bi // 16 == ai // 8) & (bi % 8 == ai % 8)
    spread = [
        dot(slots, (same & ((bi // 8) % 2 == t)).astype(F32).astype(BF16))[t : t + 1, :]
        for t in range(2)
    ]
    position = spread[0] + spread[1]
    targets = lax.broadcasted_iota(jnp.int32, (256, 256), 0).astype(F32)
    placing = (targets == position).astype(F32).astype(BF16)
    for copy in near_data + far_data:
        copy.wait_recv()
    parents = dot(placing, fbuf[...].reshape(256, features)).astype(BF16)
    pnormed = rms_rows(parents, pgv[...])
    kpv[...] = dot(pnormed, wp[:, :features]).astype(BF16)
    block = (
        lax.broadcasted_iota(jnp.int32, (features, WIN), 0) // 32 % 4
        == lax.broadcasted_iota(jnp.int32, (features, WIN), 1) // PWIN
    ).astype(F32)
    for w in range(windows):
        part = pnormed[PWIN * w : PWIN * (w + 1), :]
        repeated = jnp.concatenate([part] * 4, axis=0)
        vz[w] = (dot(wpvt[...], repeated, NT) * block).astype(BF16)

    groups = HEADS // 4
    stores = []

    def cross_scores(u):
        w, at = u // groups, 128 * (u % groups)
        keys = kpv[PWIN * w : PWIN * (w + 1), at : at + 128]
        stacked = jnp.concatenate([keys * mask for mask in head_masks], axis=0)
        return dot(stacked, qv[WIN * w : WIN * (w + 1), at : at + 128], NT)

    def cross_values(u, weights):
        w, at = u // groups, 128 * (u % groups)
        cot[w, at : at + 128, :] = dot(vz[w, at : at + 128, :], weights).astype(BF16)
        if u % groups == groups - 1:
            here = slice(WIN * w, WIN * (w + 1))
            branch = acc[here, :] + dot(jnp.transpose(cot[w]), wo[features:, :])
            ov[here, :] = (xv[here, :].astype(F32) + branch).astype(BF16)
            store = pltpu.make_async_copy(
                ov.at[pl.ds(WIN * w, WIN)], out.at[pl.ds(WIN * w, WIN)], out_sem.at[w]
            )
            store.start()
            stores.append(store)

    staged(windows * groups, PWIN, cross_scores, cross_values, sbufs, pbufs)

    to_left.wait_send()
    to_right.wait_send()
    for k in range(1, ZN):
        for copy in along_z[k]:
            copy.wait_send()
    for copy in plane:
        copy.wait_send()
    for store in stores:
        store.wait()


def on_device(
    fine_tokens,
    parent_tokens,
    shift_table,
    parent_slot,
    fine_gain,
    parent_gain,
    w_qkv,
    w_parent,
    w_out,
):
    rows, features = fine_tokens.shape
    dma = pltpu.SemaphoreType.DMA
    vmem = pltpu.VMEM
    return pl.pallas_call(
        kernel,
        out_shape=jax.ShapeDtypeStruct((rows, features), BF16),
        in_specs=[pl.BlockSpec(memory_space=pl.ANY)] * 9,
        out_specs=pl.BlockSpec(memory_space=pl.ANY),
        scratch_shapes=[
            vmem((rows, features), BF16),
            vmem((rows + 2 * HALO, features), BF16),
            vmem((2, HALO, features), BF16),
            vmem((rows, features), BF16),
            vmem((WIN, features), BF16),
            vmem((features, WIN), BF16),
            vmem((features, WIN), BF16),
            vmem((rows, features), F32),
            vmem((rows, 128), F32),
            vmem((8, 128), jnp.int32),
            vmem((1, features), F32),
            vmem((1, features), F32),
            vmem((features, 3 * features), BF16),
            vmem((features, 2 * features), BF16),
            vmem((2 * features, features), BF16),
            vmem((features, features), BF16),
            vmem((features, features), BF16),
            vmem((2, 128, features), BF16),
            vmem((2, 128, features), BF16),
            vmem((2, 128, features), BF16),
            vmem((2, 8, 1, 128), jnp.int32),
            vmem((2, 8, 8, 1, 128), jnp.int32),
            vmem((256, features), BF16),
            vmem((4, features, WIN), BF16),
            vmem((4, features, WIN), BF16),
            vmem((rows, features), BF16),
            *[vmem((WIN, WIN), F32)] * 4,
            *[vmem((WIN, WIN), BF16)] * 4,
            dma((10,)),
            dma((4,)),
            dma((2,)),
            dma((2,)),
            dma((2,)),
            dma((ZN,)),
            dma((ZN,)),
            dma((ZN,)),
            dma((ZN,)),
            dma((2, XYN)),
            dma((2, XYN)),
            dma((2, XYN)),
            dma((2, XYN)),
            pltpu.SemaphoreType.REGULAR,
        ],
        compiler_params=pltpu.CompilerParams(collective_id=0, has_side_effects=True),
    )(
        fine_tokens,
        parent_tokens,
        shift_table.reshape(8, 128),
        parent_slot.reshape(2, 1, 128),
        fine_gain.reshape(1, features),
        parent_gain.reshape(1, features),
        w_qkv,
        w_parent,
        w_out,
    )


def solution(mesh):
    return jax.shard_map(
        on_device,
        mesh=mesh,
        in_specs=(
            P(("batch", "pix"), None),
            P(("batch", "pix"), None),
            P("pix"),
            P("pix"),
            P(),
            P(),
            P(),
            P(),
            P(),
        ),
        out_specs=P(("batch", "pix"), None),
        check_vma=False,
    )
```

```python
import functools

import jax
import jax.numpy as jnp
from jax import lax
from jax.experimental import pallas as pl
from jax.experimental.pallas import tpu as pltpu
from jax.sharding import PartitionSpec as P

HEADS = 16
WIN = 256
HALO = 128
PWIN = 64
ZN = 16
XYN = 8
NEAR = (0, 1, 2, 3, 4, 13, 14, 15)
FAR = (5, 6, 7, 8, 9, 10, 11, 12)
MESH = pl.DeviceIdType.MESH
F32 = jnp.float32
BF16 = jnp.bfloat16
SCALE = 1.4426950408889634 / (32.0**0.5)

NN = (((1,), (0,)), ((), ()))
NT = (((1,), (1,)), ((), ()))
TN = (((0,), (0,)), ((), ()))


def dot(a, b, dims=NN):
    return lax.dot_general(a, b, dims, preferred_element_type=F32)


def rms_rows(rows, gain):
    values = rows.astype(F32)
    factor = lax.rsqrt(jnp.mean(values * values, axis=-1, keepdims=True) + 1e-06)
    return (values * factor * gain).astype(BF16)


def softmax_rows(scores):
    powers = jnp.exp2((scores - jnp.max(scores, axis=0, keepdims=True)) * SCALE)
    return (powers * (1.0 / jnp.sum(powers, axis=0, keepdims=True))).astype(BF16)


def staged(units, depth, scores, values, sbufs, pbufs):
    slots = len(sbufs)
    for u in range(-2, units + 2):
        if 0 <= u + 2 < units:
            sbufs[(u + 2) % slots][...] = scores(u + 2)
        if 0 <= u < units:
            for c in range(2):
                cols = slice(128 * c, 128 * (c + 1))
                for first in range(0, WIN, depth):
                    block = slice(first, first + depth)
                    pbufs[u % slots][block, cols] = softmax_rows(sbufs[u % slots][block, cols])
        if 0 <= u - 2 < units:
            values(u - 2, pbufs[(u - 2) % slots][...])


def kernel(
    fine, par, shift, pslot, fgain, pgain, wqkv, wpar, wout, out,
    xv, ext, halo, qv, kv, vt, ot, acc, relb, shv, fgv, pgv,
    wq, wp, wo, wvt, wpvt, zbuf, tbuf, fbuf, zslot, fslot, parv, xbuf, xslot, yslot, sslot, kpv, vz, cot, ov,
    s0, s1, s2, s3, p0, p1, p2, p3,
    in_sem, out_sem, own_sem, hs_sem, hr_sem, zs_sem, zr_sem, zss_sem, zsr_sem,
    ps_sem, pr_sem, pss_sem, psr_sem, far_sem,
):
    sbufs, pbufs = (s0, s1, s2, s3), (p0, p1, p2, p3)
    me = lax.axis_index("pix")
    count = ZN * XYN
    z = me // XYN
    xy = me % XYN
    right = (me + 1) % count
    left = (me + count - 1) % count
    rows = xv.shape[0]
    features = xv.shape[1]
    windows = rows // WIN
    total = rows * count

    loads = [
        pltpu.make_async_copy(fine.at[pl.ds(WIN * i, WIN)], xv.at[pl.ds(WIN * i, WIN)], in_sem.at[i])
        for i in range(4)
    ]
    loads.append(pltpu.make_async_copy(fgain, fgv, in_sem.at[4]))
    loads.append(pltpu.make_async_copy(shift, shv, in_sem.at[5]))
    loads.append(pltpu.make_async_copy(wqkv, wq, in_sem.at[6]))
    loads.append(pltpu.make_async_copy(wpar, wp, in_sem.at[7]))
    loads.append(pltpu.make_async_copy(wout, wo, in_sem.at[8]))
    loads.append(pltpu.make_async_copy(pgain, pgv, in_sem.at[9]))
    loads.append(pltpu.make_async_copy(par, parv, in_sem.at[10]))

    barrier = pltpu.get_barrier_semaphore()
    for i in (10, 0, 4, 5, 1, 2, 3, 6, 8, 7, 9):
        loads[i].start()
    peers = [((z + k) % ZN) * XYN + xy for k in NEAR[1:] + (12,)]
    peers += [z * XYN + (xy + m) % XYN for m in range(1, XYN)]
    peers += [left, right]
    for peer in peers:
        pl.semaphore_signal(barrier, inc=1, device_id={"pix": peer}, device_id_type=MESH)

    a = lax.broadcasted_iota(jnp.int32, (128, 256), 0)
    b = lax.broadcasted_iota(jnp.int32, (128, 256), 1)
    chosen = 16 * ((z + FAR[0] + (a // 2) % 8) % ZN) + 2 * (a // 16) + a % 2
    pick_far = (b == chosen).astype(F32).astype(BF16)
    loads[10].wait()
    tbuf[1] = dot(pick_far, parv[...]).astype(BF16)

    pl.semaphore_wait(barrier, len(peers))
    for k in (4, 12):
        peer = ((z + k) % ZN) * XYN + xy
        pl.semaphore_signal(far_sem, inc=1, device_id={"pix": peer}, device_id_type=MESH)

    def remote(src, dst, send, recv, peer):
        return pltpu.make_async_remote_copy(
            src_ref=src, dst_ref=dst, send_sem=send, recv_sem=recv,
            device_id={"pix": peer}, device_id_type=MESH,
        )

    to_left = remote(fine.at[pl.ds(0, HALO)], halo.at[1], hs_sem.at[0], hr_sem.at[0], left)
    to_right = remote(
        fine.at[pl.ds(rows - HALO, HALO)], halo.at[0], hs_sem.at[1], hr_sem.at[1], right
    )

    own = [
        pltpu.make_async_copy(
            par.at[pl.ds(pl.multiple_of(16 * z, 16), 16)], zbuf.at[0, pl.ds(0, 16)], own_sem.at[0]
        ),
        pltpu.make_async_copy(pslot.at[z // 8], zslot.at[0], own_sem.at[1]),
    ]
    for copy in own:
        copy.start()
    own.append(pltpu.make_async_copy(pslot, xslot.at[0], own_sem.at[2]))
    own[2].start()
    along_z = {}
    for kk, k in enumerate(NEAR):
        if k == 0:
            continue
        there = (z + k) % ZN
        peer = there * XYN + xy
        data = remote(
            par.at[pl.ds(pl.multiple_of(16 * there, 16), 16)],
            zbuf.at[0, pl.ds(16 * kk, 16)],
            zs_sem.at[k], zr_sem.at[k], peer,
        )
        slot = remote(pslot.at[there // 8], zslot.at[kk], zss_sem.at[k], zsr_sem.at[k], peer)
        along_z[k] = (data, slot)
    far_plane = []
    for m in range(1, XYN):
        there = (xy + m) % XYN
        peer = z * XYN + there
        data = remote(
            tbuf.at[1, pl.ds(pl.multiple_of(16 * there, 16), 16)],
            zbuf.at[1, pl.ds(16 * m, 16)],
            ps_sem.at[1, m], pr_sem.at[1, m], peer,
        )
        slot = remote(pslot, xslot.at[m], pss_sem.at[1, m], psr_sem.at[1, m], peer)
        far_plane.append((data, slot))
    for i, k in enumerate((4, 12 + 1, 3, 14, 2, 15, 1)):
        far_plane[i][1].start()
        far_plane[i][0].start()
        along_z[k][1].start()
        along_z[k][0].start()
    to_left.start()
    to_right.start()

    loads[4].wait()
    loads[5].wait()
    place = lax.broadcasted_iota(jnp.int32, (8, 128), 0) * 128 + lax.broadcasted_iota(
        jnp.int32, (8, 128), 1
    )
    away = shv[...] - (place + me * rows)
    away = jnp.where(away > total // 2, away - total, away)
    away = jnp.where(away < -(total // 2), away + total, away)
    rel = ((place % WIN) + away + HALO).astype(F32)
    for i in range(8):
        relb[128 * i : 128 * (i + 1), :] = jnp.transpose(
            jnp.broadcast_to(rel[i : i + 1, :], (128, 128))
        )
    gain = fgv[...]
    for i in range(4):
        loads[i].wait()

        def norm_step(s, carry):
            at = pl.multiple_of(WIN * i + 64 * s, 64)
            ext[pl.ds(pl.multiple_of(at + HALO, 64), 64), :] = rms_rows(xv[pl.ds(at, 64), :], gain)
            return carry

        lax.fori_loop(0, WIN // 64, norm_step, 0)
    loads[6].wait()
    wvt[...] = jnp.transpose(wq[:, 2 * features :])

    for data, slot in far_plane:
        data.wait_recv()
        slot.wait_recv()
    own[2].wait()
    zbuf[1, 0:16, :] = tbuf[1, pl.ds(pl.multiple_of(16 * xy, 16), 16), :]
    a = lax.broadcasted_iota(jnp.int32, (128, 128), 0)
    b = lax.broadcasted_iota(jnp.int32, (128, 128), 1)
    order = (b == (a % 8) * 16 + (a // 16) * 2 + (a // 8) % 2).astype(F32).astype(BF16)
    xbuf[...] = dot(order, zbuf[1]).astype(BF16)
    tables = xslot[...].reshape(16, 128).astype(F32)
    tables = tables.reshape(8, 2, 128)
    tables = jnp.concatenate([tables[:, 0, :], tables[:, 1, :]], axis=1)
    ka = lax.broadcasted_iota(jnp.int32, (8, 256), 0)
    kb = lax.broadcasted_iota(jnp.int32, (8, 256), 1)
    slots = None
    for t in range(2):
        hit = (kb == 16 * ((z + FAR[0] + ka) % ZN) + 2 * xy + t).astype(F32).astype(BF16)
        parts = [jnp.zeros((8, 256), F32)] * 16
        parts[t] = tables
        part = dot(hit, jnp.concatenate(parts, axis=0).astype(BF16), NT)
        slots = part if slots is None else slots + part
    for kk in range(8):
        yslot[kk] = slots[kk : kk + 1, :]
    far_z = []
    for kk, k in enumerate(FAR):
        peer = ((z + k) % ZN) * XYN + xy
        data = remote(
            xbuf.at[pl.ds(16 * kk, 16)], fbuf.at[1, pl.ds(16 * kk, 16)],
            zs_sem.at[k], zr_sem.at[k], peer,
        )
        slot = remote(yslot.at[kk], sslot.at[kk], zss_sem.at[k], zsr_sem.at[k], peer)
        far_z.append((data, slot))
    pl.semaphore_wait(far_sem, 2)
    for i in (3, 4, 2, 5, 1, 6, 0, 7):
        far_z[i][1].start()
        far_z[i][0].start()

    lanes128 = lax.broadcasted_iota(jnp.int32, (1, 128), 1)
    lane_rows = lax.broadcasted_iota(jnp.int32, (WIN, 128), 1).astype(F32)
    head_masks = [(lanes128 // 32 == t).astype(F32).astype(BF16) for t in range(4)]

    def window(i, carry):
        w = (i + 1) % windows
        base = pl.multiple_of(w * WIN, WIN)
        own_rows = ext[pl.ds(pl.multiple_of(base + HALO, HALO), WIN), :]
        qv[pl.ds(base, WIN), :] = dot(own_rows, wq[:, :features]).astype(BF16)
        where = relb[pl.ds(base, WIN), :]
        picks = jnp.concatenate(
            [(where == lane_rows + 128.0 * c).astype(F32).astype(BF16) for c in range(4)], axis=1
        )
        gathered = dot(picks, ext[pl.ds(base, 2 * WIN), :]).astype(BF16)
        kv[...] = dot(gathered, wq[:, features : 2 * features]).astype(BF16)
        vt[...] = dot(wvt[...], gathered, NT).astype(BF16)

        def self_scores(h):
            at = 128 * (h // 4)
            keys = kv[:, at : at + 128] * head_masks[h % 4]
            return dot(keys, qv[pl.ds(base, WIN), at : at + 128], NT)

        def self_values(h, weights):
            ot[32 * h : 32 * h + 32, :] = dot(vt[32 * h : 32 * h + 32, :], weights).astype(BF16)

        staged(HEADS, WIN, self_scores, self_values, sbufs, pbufs)
        acc[pl.ds(base, WIN), :] = dot(jnp.transpose(ot[...]), wo[:features, :])
        return carry

    def near_phase():
        for k in NEAR:
            if k == 0:
                own[1].wait()
            else:
                along_z[k][1].wait_recv()
        slots = [
            remote(
                zslot, fslot.at[m], pss_sem.at[0, m], psr_sem.at[0, m],
                z * XYN + (xy + m) % XYN,
            )
            for m in range(1, XYN)
        ]
        for copy in slots:
            copy.start()
        for k in NEAR:
            if k == 0:
                own[0].wait()
            else:
                along_z[k][0].wait_recv()
        tbuf[0] = dot(order, zbuf[0]).astype(BF16)
        fslot[0] = zslot[...]
        fbuf[0, 0:16, :] = tbuf[0, pl.ds(pl.multiple_of(16 * xy, 16), 16), :]
        data = []
        for m in range(1, XYN):
            there = (xy + m) % XYN
            data.append(
                remote(
                    tbuf.at[0, pl.ds(pl.multiple_of(16 * there, 16), 16)],
                    fbuf.at[0, pl.ds(16 * m, 16)],
                    ps_sem.at[0, m], pr_sem.at[0, m], z * XYN + there,
                )
            )
        for copy in data:
            copy.start()
        return data, slots

    loads[8].wait()
    lax.fori_loop(0, 1, window, 0)
    near_data, near_slots = near_phase()
    lax.fori_loop(1, 2, window, 0)

    to_left.wait_recv()
    to_right.wait_recv()
    ext[:HALO, :] = rms_rows(halo[0], gain)
    ext[HALO + rows :, :] = rms_rows(halo[1], gain)
    lax.fori_loop(2, 4, window, 0)

    loads[7].wait()
    loads[9].wait()
    wpvt[...] = jnp.transpose(wp[:, features:])

    for copy in near_slots:
        copy.wait_recv()
    table = jnp.concatenate([fslot[...].reshape(64, 128).astype(F32), jnp.zeros((64, 128), F32)], axis=0)
    first = 16 * (z % 8) + 2 * xy
    wanted = lax.broadcasted_iota(jnp.int32, (8, 128), 0) + first
    select = (lax.broadcasted_iota(jnp.int32, (8, 128), 1) == wanted).astype(F32).astype(BF16)
    slots = dot(select, table.astype(BF16), NT).astype(BF16)
    same = (b // 16 == a // 8) & (b % 8 == a % 8)
    spread = [
        dot(slots, (same & ((b // 8) % 2 == t)).astype(F32).astype(BF16))[t : t + 1, :]
        for t in range(2)
    ]
    near_position = spread[0] + spread[1]
    for data, slot in far_z:
        slot.wait_recv()
    slots = dot(
        sslot[...].reshape(8, 128).astype(BF16), (a == b % 16).astype(F32).astype(BF16)
    )
    held = lax.broadcasted_iota(jnp.int32, (8, 128), 1) // 16 == lax.broadcasted_iota(
        jnp.int32, (8, 128), 0
    )
    far_position = jnp.sum(jnp.where(held, slots, 0.0), axis=0, keepdims=True)
    position = jnp.concatenate([near_position, far_position], axis=1)
    targets = lax.broadcasted_iota(jnp.int32, (256, 256), 0).astype(F32)
    placing = (targets == position).astype(F32).astype(BF16)
    for copy in near_data + [data for data, slot in far_z]:
        copy.wait_recv()
    parents = dot(placing, fbuf[...].reshape(256, features)).astype(BF16)
    pnormed = rms_rows(parents, pgv[...])
    kpv[...] = dot(pnormed, wp[:, :features]).astype(BF16)
    block = (
        lax.broadcasted_iota(jnp.int32, (features, WIN), 0) // 32 % 4
        == lax.broadcasted_iota(jnp.int32, (features, WIN), 1) // PWIN
    ).astype(F32)
    for w in range(windows):
        part = pnormed[PWIN * w : PWIN * (w + 1), :]
        repeated = jnp.concatenate([part] * 4, axis=0)
        vz[w] = (dot(wpvt[...], repeated, NT) * block).astype(BF16)

    groups = HEADS // 4
    stores = []

    def cross_scores(u):
        w, at = u // groups, 128 * (u % groups)
        keys = kpv[PWIN * w : PWIN * (w + 1), at : at + 128]
        stacked = jnp.concatenate([keys * mask for mask in head_masks], axis=0)
        return dot(stacked, qv[WIN * w : WIN * (w + 1), at : at + 128], NT)

    def cross_values(u, weights):
        w, at = u // groups, 128 * (u % groups)
        cot[w, at : at + 128, :] = dot(vz[w, at : at + 128, :], weights).astype(BF16)
        if u % groups == groups - 1:
            here = slice(WIN * w, WIN * (w + 1))
            branch = acc[here, :] + dot(jnp.transpose(cot[w]), wo[features:, :])
            ov[here, :] = (xv[here, :].astype(F32) + branch).astype(BF16)
            store = pltpu.make_async_copy(
                ov.at[pl.ds(WIN * w, WIN)], out.at[pl.ds(WIN * w, WIN)], out_sem.at[w]
            )
            store.start()
            stores.append(store)

    staged(windows * groups, PWIN, cross_scores, cross_values, sbufs, pbufs)

    to_left.wait_send()
    to_right.wait_send()
    for pair in list(along_z.values()) + far_plane + far_z:
        for copy in pair:
            copy.wait_send()
    for copy in near_data + near_slots:
        copy.wait_send()
    for store in stores:
        store.wait()


def on_device(
    fine_tokens,
    parent_tokens,
    shift_table,
    parent_slot,
    fine_gain,
    parent_gain,
    w_qkv,
    w_parent,
    w_out,
):
    rows, features = fine_tokens.shape
    dma = pltpu.SemaphoreType.DMA
    vmem = pltpu.VMEM
    return pl.pallas_call(
        kernel,
        out_shape=jax.ShapeDtypeStruct((rows, features), BF16),
        in_specs=[pl.BlockSpec(memory_space=pl.ANY)] * 9,
        out_specs=pl.BlockSpec(memory_space=pl.ANY),
        scratch_shapes=[
            vmem((rows, features), BF16),
            vmem((rows + 2 * HALO, features), BF16),
            vmem((2, HALO, features), BF16),
            vmem((rows, features), BF16),
            vmem((WIN, features), BF16),
            vmem((features, WIN), BF16),
            vmem((features, WIN), BF16),
            vmem((rows, features), F32),
            vmem((rows, 128), F32),
            vmem((8, 128), jnp.int32),
            vmem((1, features), F32),
            vmem((1, features), F32),
            vmem((features, 3 * features), BF16),
            vmem((features, 2 * features), BF16),
            vmem((2 * features, features), BF16),
            vmem((features, features), BF16),
            vmem((features, features), BF16),
            vmem((2, 128, features), BF16),
            vmem((2, 128, features), BF16),
            vmem((2, 128, features), BF16),
            vmem((8, 1, 128), jnp.int32),
            vmem((8, 8, 1, 128), jnp.int32),
            vmem((256, features), BF16),
            vmem((128, features), BF16),
            vmem((8, 2, 1, 128), jnp.int32),
            vmem((8, 1, 128), F32),
            vmem((8, 1, 128), F32),
            vmem((256, features), BF16),
            vmem((4, features, WIN), BF16),
            vmem((4, features, WIN), BF16),
            vmem((rows, features), BF16),
            *[vmem((WIN, WIN), F32)] * 4,
            *[vmem((WIN, WIN), BF16)] * 4,
            dma((11,)),
            dma((4,)),
            dma((3,)),
            dma((2,)),
            dma((2,)),
            dma((ZN,)),
            dma((ZN,)),
            dma((ZN,)),
            dma((ZN,)),
            dma((2, XYN)),
            dma((2, XYN)),
            dma((2, XYN)),
            dma((2, XYN)),
            pltpu.SemaphoreType.REGULAR,
        ],
        compiler_params=pltpu.CompilerParams(collective_id=0, has_side_effects=True),
    )(
        fine_tokens,
        parent_tokens,
        shift_table.reshape(8, 128),
        parent_slot.reshape(2, 1, 128),
        fine_gain.reshape(1, features),
        parent_gain.reshape(1, features),
        w_qkv,
        w_parent,
        w_out,
    )


def solution(mesh):
    return jax.shard_map(
        on_device,
        mesh=mesh,
        in_specs=(
            P(("batch", "pix"), None),
            P(("batch", "pix"), None),
            P("pix"),
            P("pix"),
            P(),
            P(),
            P(),
            P(),
            P(),
        ),
        out_specs=P(("batch", "pix"), None),
        check_vma=False,
    )
```

```python
import functools

import jax
import jax.numpy as jnp
from jax import lax
from jax.experimental import pallas as pl
from jax.experimental.pallas import tpu as pltpu
from jax.sharding import PartitionSpec as P

HEADS = 16
WIN = 256
HALO = 128
PWIN = 64
ZN = 16
XYN = 8
NEAR = (0, 1, 2, 3, 4, 13, 14, 15)
FAR = (5, 6, 7, 8, 9, 10, 11, 12)
MESH = pl.DeviceIdType.MESH
F32 = jnp.float32
BF16 = jnp.bfloat16
SCALE = 1.4426950408889634 / (32.0**0.5)

NN = (((1,), (0,)), ((), ()))
NT = (((1,), (1,)), ((), ()))
TN = (((0,), (0,)), ((), ()))


def dot(a, b, dims=NN):
    return lax.dot_general(a, b, dims, preferred_element_type=F32)


def rms_rows(rows, gain):
    values = rows.astype(F32)
    factor = lax.rsqrt(jnp.mean(values * values, axis=-1, keepdims=True) + 1e-06)
    return (values * factor * gain).astype(BF16)


def softmax_rows(scores):
    powers = jnp.exp2((scores - jnp.max(scores, axis=0, keepdims=True)) * SCALE)
    return (powers * (1.0 / jnp.sum(powers, axis=0, keepdims=True))).astype(BF16)


def staged(units, depth, scores, values, sbufs, pbufs):
    slots = len(sbufs)
    for u in range(-2, units + 2):
        if 0 <= u + 2 < units:
            sbufs[(u + 2) % slots][...] = scores(u + 2)
        if 0 <= u < units:
            for c in range(2):
                cols = slice(128 * c, 128 * (c + 1))
                for first in range(0, WIN, depth):
                    block = slice(first, first + depth)
                    pbufs[u % slots][block, cols] = softmax_rows(sbufs[u % slots][block, cols])
        if 0 <= u - 2 < units:
            values(u - 2, pbufs[(u - 2) % slots][...])


def kernel(
    fine, par, shift, pslot, fgain, pgain, wqkv, wpar, out,
    xv, ext, halo, qv, kv, vt, ot, relb, shv, fgv, pgv,
    wq, wp, wvt, zbuf, tbuf, fbuf, zslot, fslot, parv, xbuf, xslot, yslot, sslot, kpv, cot, ov,
    s0, s1, s2, s3, p0, p1, p2, p3,
    in_sem, out_sem, own_sem, hs_sem, hr_sem, zs_sem, zr_sem, zss_sem, zsr_sem,
    ps_sem, pr_sem, pss_sem, psr_sem, far_sem,
):
    sbufs, pbufs = (s0, s1, s2, s3), (p0, p1, p2, p3)
    me = lax.axis_index("pix")
    count = ZN * XYN
    z = me // XYN
    xy = me % XYN
    right = (me + 1) % count
    left = (me + count - 1) % count
    rows = xv.shape[0]
    features = xv.shape[1]
    windows = rows // WIN
    total = rows * count

    loads = [
        pltpu.make_async_copy(fine.at[pl.ds(WIN * i, WIN)], xv.at[pl.ds(WIN * i, WIN)], in_sem.at[i])
        for i in range(4)
    ]
    loads.append(pltpu.make_async_copy(fgain, fgv, in_sem.at[4]))
    loads.append(pltpu.make_async_copy(shift, shv, in_sem.at[5]))
    loads.append(pltpu.make_async_copy(wqkv, wq, in_sem.at[6]))
    loads.append(pltpu.make_async_copy(wpar, wp, in_sem.at[7]))
    loads.append(pltpu.make_async_copy(pgain, pgv, in_sem.at[8]))
    loads.append(pltpu.make_async_copy(par, parv, in_sem.at[9]))

    barrier = pltpu.get_barrier_semaphore()
    for i in (9, 0, 4, 5, 1, 2, 3, 6, 7, 8):
        loads[i].start()
    peers = [((z + k) % ZN) * XYN + xy for k in NEAR[1:] + (12,)]
    peers += [z * XYN + (xy + m) % XYN for m in range(1, XYN)]
    peers += [left, right]
    for peer in peers:
        pl.semaphore_signal(barrier, inc=1, device_id={"pix": peer}, device_id_type=MESH)

    a = lax.broadcasted_iota(jnp.int32, (128, 256), 0)
    b = lax.broadcasted_iota(jnp.int32, (128, 256), 1)
    chosen = 16 * ((z + FAR[0] + (a // 2) % 8) % ZN) + 2 * (a // 16) + a % 2
    pick_far = (b == chosen).astype(F32).astype(BF16)
    loads[9].wait()
    tbuf[1] = dot(pick_far, parv[...]).astype(BF16)

    pl.semaphore_wait(barrier, len(peers))
    for k in (4, 12):
        peer = ((z + k) % ZN) * XYN + xy
        pl.semaphore_signal(far_sem, inc=1, device_id={"pix": peer}, device_id_type=MESH)

    def remote(src, dst, send, recv, peer):
        return pltpu.make_async_remote_copy(
            src_ref=src, dst_ref=dst, send_sem=send, recv_sem=recv,
            device_id={"pix": peer}, device_id_type=MESH,
        )

    to_left = remote(fine.at[pl.ds(0, HALO)], halo.at[1], hs_sem.at[0], hr_sem.at[0], left)
    to_right = remote(
        fine.at[pl.ds(rows - HALO, HALO)], halo.at[0], hs_sem.at[1], hr_sem.at[1], right
    )

    own = [
        pltpu.make_async_copy(
            par.at[pl.ds(pl.multiple_of(16 * z, 16), 16)], zbuf.at[0, pl.ds(0, 16)], own_sem.at[0]
        ),
        pltpu.make_async_copy(pslot.at[z // 8], zslot.at[0], own_sem.at[1]),
    ]
    for copy in own:
        copy.start()
    own.append(pltpu.make_async_copy(pslot, xslot.at[0], own_sem.at[2]))
    own[2].start()
    along_z = {}
    for kk, k in enumerate(NEAR):
        if k == 0:
            continue
        there = (z + k) % ZN
        peer = there * XYN + xy
        data = remote(
            par.at[pl.ds(pl.multiple_of(16 * there, 16), 16)],
            zbuf.at[0, pl.ds(16 * kk, 16)],
            zs_sem.at[k], zr_sem.at[k], peer,
        )
        slot = remote(pslot.at[there // 8], zslot.at[kk], zss_sem.at[k], zsr_sem.at[k], peer)
        along_z[k] = (data, slot)
    far_plane = []
    for m in range(1, XYN):
        there = (xy + m) % XYN
        peer = z * XYN + there
        data = remote(
            tbuf.at[1, pl.ds(pl.multiple_of(16 * there, 16), 16)],
            zbuf.at[1, pl.ds(16 * m, 16)],
            ps_sem.at[1, m], pr_sem.at[1, m], peer,
        )
        slot = remote(pslot, xslot.at[m], pss_sem.at[1, m], psr_sem.at[1, m], peer)
        far_plane.append((data, slot))
    for i, k in enumerate((4, 12 + 1, 3, 14, 2, 15, 1)):
        far_plane[i][1].start()
        far_plane[i][0].start()
        along_z[k][1].start()
        along_z[k][0].start()
    to_left.start()
    to_right.start()

    loads[4].wait()
    loads[5].wait()
    place = lax.broadcasted_iota(jnp.int32, (8, 128), 0) * 128 + lax.broadcasted_iota(
        jnp.int32, (8, 128), 1
    )
    away = shv[...] - (place + me * rows)
    away = jnp.where(away > total // 2, away - total, away)
    away = jnp.where(away < -(total // 2), away + total, away)
    rel = ((place % WIN) + away + HALO).astype(F32)
    for i in range(8):
        relb[128 * i : 128 * (i + 1), :] = jnp.transpose(
            jnp.broadcast_to(rel[i : i + 1, :], (128, 128))
        )
    gain = fgv[...]
    for i in range(4):
        loads[i].wait()

        def norm_step(s, carry):
            at = pl.multiple_of(WIN * i + 64 * s, 64)
            ext[pl.ds(pl.multiple_of(at + HALO, 64), 64), :] = rms_rows(xv[pl.ds(at, 64), :], gain)
            return carry

        lax.fori_loop(0, WIN // 64, norm_step, 0)
    loads[6].wait()
    wvt[...] = jnp.transpose(wq[:, 2 * features :])

    for data, slot in far_plane:
        data.wait_recv()
        slot.wait_recv()
    own[2].wait()
    zbuf[1, 0:16, :] = tbuf[1, pl.ds(pl.multiple_of(16 * xy, 16), 16), :]
    a = lax.broadcasted_iota(jnp.int32, (128, 128), 0)
    b = lax.broadcasted_iota(jnp.int32, (128, 128), 1)
    order = (b == (a % 8) * 16 + (a // 16) * 2 + (a // 8) % 2).astype(F32).astype(BF16)
    xbuf[...] = dot(order, zbuf[1]).astype(BF16)
    tables = xslot[...].reshape(16, 128).astype(F32)
    tables = tables.reshape(8, 2, 128)
    tables = jnp.concatenate([tables[:, 0, :], tables[:, 1, :]], axis=1)
    ka = lax.broadcasted_iota(jnp.int32, (8, 256), 0)
    kb = lax.broadcasted_iota(jnp.int32, (8, 256), 1)
    slots = None
    for t in range(2):
        hit = (kb == 16 * ((z + FAR[0] + ka) % ZN) + 2 * xy + t).astype(F32).astype(BF16)
        parts = [jnp.zeros((8, 256), F32)] * 16
        parts[t] = tables
        part = dot(hit, jnp.concatenate(parts, axis=0).astype(BF16), NT)
        slots = part if slots is None else slots + part
    for kk in range(8):
        yslot[kk] = slots[kk : kk + 1, :]
    far_z = []
    for kk, k in enumerate(FAR):
        peer = ((z + k) % ZN) * XYN + xy
        data = remote(
            xbuf.at[pl.ds(16 * kk, 16)], fbuf.at[1, pl.ds(16 * kk, 16)],
            zs_sem.at[k], zr_sem.at[k], peer,
        )
        slot = remote(yslot.at[kk], sslot.at[kk], zss_sem.at[k], zsr_sem.at[k], peer)
        far_z.append((data, slot))
    pl.semaphore_wait(far_sem, 2)
    for i in (3, 4, 2, 5, 1, 6, 0, 7):
        far_z[i][1].start()
        far_z[i][0].start()

    lanes128 = lax.broadcasted_iota(jnp.int32, (1, 128), 1)
    lane_rows = lax.broadcasted_iota(jnp.int32, (WIN, 128), 1).astype(F32)
    head_masks = [(lanes128 // 32 == t).astype(F32).astype(BF16) for t in range(4)]

    def window(i, carry):
        w = (i + 1) % windows
        base = pl.multiple_of(w * WIN, WIN)
        own_rows = ext[pl.ds(pl.multiple_of(base + HALO, HALO), WIN), :]
        qv[pl.ds(base, WIN), :] = dot(own_rows, wq[:, :features]).astype(BF16)
        where = relb[pl.ds(base, WIN), :]
        picks = jnp.concatenate(
            [(where == lane_rows + 128.0 * c).astype(F32).astype(BF16) for c in range(4)], axis=1
        )
        gathered = dot(picks, ext[pl.ds(base, 2 * WIN), :]).astype(BF16)
        kv[...] = dot(gathered, wq[:, features : 2 * features]).astype(BF16)
        vt[...] = dot(wvt[...], gathered, NT).astype(BF16)

        def self_scores(h):
            at = 128 * (h // 4)
            keys = kv[:, at : at + 128] * head_masks[h % 4]
            return dot(keys, qv[pl.ds(base, WIN), at : at + 128], NT)

        def self_values(h, weights):
            ot[32 * h : 32 * h + 32, :] = dot(vt[32 * h : 32 * h + 32, :], weights).astype(BF16)

        staged(HEADS, WIN, self_scores, self_values, sbufs, pbufs)
        ov[pl.ds(base, WIN), :features] = jnp.transpose(ot[...])
        return carry

    def near_phase():
        for k in NEAR:
            if k == 0:
                own[1].wait()
            else:
                along_z[k][1].wait_recv()
        slots = [
            remote(
                zslot, fslot.at[m], pss_sem.at[0, m], psr_sem.at[0, m],
                z * XYN + (xy + m) % XYN,
            )
            for m in range(1, XYN)
        ]
        for copy in slots:
            copy.start()
        for k in NEAR:
            if k == 0:
                own[0].wait()
            else:
                along_z[k][0].wait_recv()
        tbuf[0] = dot(order, zbuf[0]).astype(BF16)
        fslot[0] = zslot[...]
        fbuf[0, 0:16, :] = tbuf[0, pl.ds(pl.multiple_of(16 * xy, 16), 16), :]
        data = []
        for m in range(1, XYN):
            there = (xy + m) % XYN
            data.append(
                remote(
                    tbuf.at[0, pl.ds(pl.multiple_of(16 * there, 16), 16)],
                    fbuf.at[0, pl.ds(16 * m, 16)],
                    ps_sem.at[0, m], pr_sem.at[0, m], z * XYN + there,
                )
            )
        for copy in data:
            copy.start()
        return data, slots

    lax.fori_loop(0, 1, window, 0)
    near_data, near_slots = near_phase()
    lax.fori_loop(1, 2, window, 0)

    to_left.wait_recv()
    to_right.wait_recv()
    ext[:HALO, :] = rms_rows(halo[0], gain)
    ext[HALO + rows :, :] = rms_rows(halo[1], gain)
    lax.fori_loop(2, 4, window, 0)

    self_store = pltpu.make_async_copy(
        ov.at[:, pl.ds(0, features)], out.at[:, pl.ds(0, features)], out_sem.at[4]
    )
    self_store.start()
    stores = [self_store]
    loads[7].wait()
    loads[8].wait()

    for copy in near_slots:
        copy.wait_recv()
    table = jnp.concatenate([fslot[...].reshape(64, 128).astype(F32), jnp.zeros((64, 128), F32)], axis=0)
    first = 16 * (z % 8) + 2 * xy
    wanted = lax.broadcasted_iota(jnp.int32, (8, 128), 0) + first
    select = (lax.broadcasted_iota(jnp.int32, (8, 128), 1) == wanted).astype(F32).astype(BF16)
    slots = dot(select, table.astype(BF16), NT).astype(BF16)
    same = (b // 16 == a // 8) & (b % 8 == a % 8)
    spread = [
        dot(slots, (same & ((b // 8) % 2 == t)).astype(F32).astype(BF16))[t : t + 1, :]
        for t in range(2)
    ]
    near_position = spread[0] + spread[1]
    for data, slot in far_z:
        slot.wait_recv()
    slots = dot(
        sslot[...].reshape(8, 128).astype(BF16), (a == b % 16).astype(F32).astype(BF16)
    )
    held = lax.broadcasted_iota(jnp.int32, (8, 128), 1) // 16 == lax.broadcasted_iota(
        jnp.int32, (8, 128), 0
    )
    far_position = jnp.sum(jnp.where(held, slots, 0.0), axis=0, keepdims=True)
    position = jnp.concatenate([near_position, far_position], axis=1)
    targets = lax.broadcasted_iota(jnp.int32, (256, 256), 0).astype(F32)
    placing = (targets == position).astype(F32).astype(BF16)
    for copy in near_data + [data for data, slot in far_z]:
        copy.wait_recv()
    parents = dot(placing, fbuf[...].reshape(256, features)).astype(BF16)
    pnormed = rms_rows(parents, pgv[...])
    kpv[...] = dot(pnormed, wp[...]).astype(BF16)
    groups = HEADS // 4

    def cross_scores(u):
        w, at = u // groups, 128 * (u % groups)
        keys = kpv[PWIN * w : PWIN * (w + 1), at : at + 128]
        stacked = jnp.concatenate([keys * mask for mask in head_masks], axis=0)
        return dot(stacked, qv[WIN * w : WIN * (w + 1), at : at + 128], NT)

    def cross_values(u, weights):
        w, at = u // groups, 128 * (u % groups)
        part = kpv[PWIN * w : PWIN * (w + 1), features + at : features + at + 128]
        stacked = jnp.concatenate([part * mask for mask in head_masks], axis=0)
        cot[w, at : at + 128, :] = dot(stacked, weights, TN).astype(BF16)
        if u % groups == groups - 1:
            here = slice(WIN * w, WIN * (w + 1))
            ov[here, features:] = jnp.transpose(cot[w])
            store = pltpu.make_async_copy(
                ov.at[pl.ds(WIN * w, WIN), pl.ds(features, features)],
                out.at[pl.ds(WIN * w, WIN), pl.ds(features, features)],
                out_sem.at[w],
            )
            store.start()
            stores.append(store)

    staged(windows * groups, PWIN, cross_scores, cross_values, sbufs, pbufs)

    to_left.wait_send()
    to_right.wait_send()
    for pair in list(along_z.values()) + far_plane + far_z:
        for copy in pair:
            copy.wait_send()
    for copy in near_data + near_slots:
        copy.wait_send()
    for store in stores:
        store.wait()


def on_device(
    fine_tokens,
    parent_tokens,
    shift_table,
    parent_slot,
    fine_gain,
    parent_gain,
    w_qkv,
    w_parent,
    w_out,
):
    rows, features = fine_tokens.shape
    dma = pltpu.SemaphoreType.DMA
    vmem = pltpu.VMEM
    joined = pl.pallas_call(
        kernel,
        out_shape=jax.ShapeDtypeStruct((rows, 2 * features), BF16),
        in_specs=[pl.BlockSpec(memory_space=pl.ANY)] * 8,
        out_specs=pl.BlockSpec(memory_space=pl.ANY),
        scratch_shapes=[
            vmem((rows, features), BF16),
            vmem((rows + 2 * HALO, features), BF16),
            vmem((2, HALO, features), BF16),
            vmem((rows, features), BF16),
            vmem((WIN, features), BF16),
            vmem((features, WIN), BF16),
            vmem((features, WIN), BF16),
            vmem((rows, 128), F32),
            vmem((8, 128), jnp.int32),
            vmem((1, features), F32),
            vmem((1, features), F32),
            vmem((features, 3 * features), BF16),
            vmem((features, 2 * features), BF16),
            vmem((features, features), BF16),
            vmem((2, 128, features), BF16),
            vmem((2, 128, features), BF16),
            vmem((2, 128, features), BF16),
            vmem((8, 1, 128), jnp.int32),
            vmem((8, 8, 1, 128), jnp.int32),
            vmem((256, features), BF16),
            vmem((128, features), BF16),
            vmem((8, 2, 1, 128), jnp.int32),
            vmem((8, 1, 128), F32),
            vmem((8, 1, 128), F32),
            vmem((256, 2 * features), BF16),
            vmem((4, features, WIN), BF16),
            vmem((rows, 2 * features), BF16),
            *[vmem((WIN, WIN), F32)] * 4,
            *[vmem((WIN, WIN), BF16)] * 4,
            dma((10,)),
            dma((5,)),
            dma((3,)),
            dma((2,)),
            dma((2,)),
            dma((ZN,)),
            dma((ZN,)),
            dma((ZN,)),
            dma((ZN,)),
            dma((2, XYN)),
            dma((2, XYN)),
            dma((2, XYN)),
            dma((2, XYN)),
            pltpu.SemaphoreType.REGULAR,
        ],
        compiler_params=pltpu.CompilerParams(collective_id=0, has_side_effects=True, vmem_limit_bytes=25165824),
    )(
        *[
            pltpu.with_memory_space_constraint(x, pltpu.HBM)
            for x in (
                fine_tokens,
                parent_tokens,
                shift_table.reshape(8, 128),
                parent_slot.reshape(2, 1, 128),
                fine_gain.reshape(1, features),
                parent_gain.reshape(1, features),
                w_qkv,
                w_parent,
            )
        ]
    )
    branch = jnp.dot(joined, w_out, preferred_element_type=F32)
    return (fine_tokens.astype(F32) + branch).astype(BF16)


def solution(mesh):
    return jax.shard_map(
        on_device,
        mesh=mesh,
        in_specs=(
            P(("batch", "pix"), None),
            P(("batch", "pix"), None),
            P("pix"),
            P("pix"),
            P(),
            P(),
            P(),
            P(),
            P(),
        ),
        out_specs=P(("batch", "pix"), None),
        check_vma=False,
    )
```

```python
import functools

import jax
import jax.numpy as jnp
from jax import lax
from jax.experimental import pallas as pl
from jax.experimental.pallas import tpu as pltpu
from jax.sharding import PartitionSpec as P

HEADS = 16
WIN = 256
HALO = 128
PWIN = 64
ZN = 16
XYN = 8
NEAR = (0, 1, 2, 3, 4, 13, 14, 15)
FAR = (5, 6, 7, 8, 9, 10, 11, 12)
MESH = pl.DeviceIdType.MESH
F32 = jnp.float32
BF16 = jnp.bfloat16
SCALE = 1.4426950408889634 / (32.0**0.5)

NN = (((1,), (0,)), ((), ()))
NT = (((1,), (1,)), ((), ()))
TN = (((0,), (0,)), ((), ()))


def dot(a, b, dims=NN):
    return lax.dot_general(a, b, dims, preferred_element_type=F32)


def rms_rows(rows, gain):
    values = rows.astype(F32)
    factor = lax.rsqrt(jnp.mean(values * values, axis=-1, keepdims=True) + 1e-06)
    return (values * factor * gain).astype(BF16)


def softmax_rows(scores):
    powers = jnp.exp2((scores - jnp.max(scores, axis=0, keepdims=True)) * SCALE)
    return (powers * (1.0 / jnp.sum(powers, axis=0, keepdims=True))).astype(BF16)


def staged(units, depth, scores, values, sbufs, pbufs):
    slots = len(sbufs)
    for u in range(-2, units + 2):
        if 0 <= u + 2 < units:
            sbufs[(u + 2) % slots][...] = scores(u + 2)
        if 0 <= u < units:
            for c in range(2):
                cols = slice(128 * c, 128 * (c + 1))
                for first in range(0, WIN, depth):
                    block = slice(first, first + depth)
                    pbufs[u % slots][block, cols] = softmax_rows(sbufs[u % slots][block, cols])
        if 0 <= u - 2 < units:
            values(u - 2, pbufs[(u - 2) % slots][...])


def kernel(
    fine, par, shift, pslot, fgain, pgain, wqkv, wpar, out,
    xv, ext, halo, qv, kv, vt, ot, relb, shv, fgv, pgv,
    wq, wp, wvt, zbuf, tbuf, fbuf, zslot, fslot, parv, xbuf, xslot, yslot, sslot, kpv, cot,
    s0, s1, s2, s3, p0, p1, p2, p3,
    in_sem, own_sem, hs_sem, hr_sem, zs_sem, zr_sem, zss_sem, zsr_sem,
    ps_sem, pr_sem, pss_sem, psr_sem, far_sem,
):
    sbufs, pbufs = (s0, s1, s2, s3), (p0, p1, p2, p3)
    me = lax.axis_index("pix")
    count = ZN * XYN
    z = me // XYN
    xy = me % XYN
    right = (me + 1) % count
    left = (me + count - 1) % count
    rows = xv.shape[0]
    features = xv.shape[1]
    windows = rows // WIN
    total = rows * count

    loads = [
        pltpu.make_async_copy(fine.at[pl.ds(WIN * i, WIN)], xv.at[pl.ds(WIN * i, WIN)], in_sem.at[i])
        for i in range(4)
    ]
    loads.append(pltpu.make_async_copy(fgain, fgv, in_sem.at[4]))
    loads.append(pltpu.make_async_copy(shift, shv, in_sem.at[5]))
    loads.append(pltpu.make_async_copy(wqkv, wq, in_sem.at[6]))
    loads.append(pltpu.make_async_copy(wpar, wp, in_sem.at[7]))
    loads.append(pltpu.make_async_copy(pgain, pgv, in_sem.at[8]))
    loads.append(pltpu.make_async_copy(par, parv, in_sem.at[9]))

    barrier = pltpu.get_barrier_semaphore()
    for i in (9, 0, 4, 5, 1, 2, 3, 6, 7, 8):
        loads[i].start()
    peers = [((z + k) % ZN) * XYN + xy for k in NEAR[1:] + (12,)]
    peers += [z * XYN + (xy + m) % XYN for m in range(1, XYN)]
    peers += [left, right]
    for peer in peers:
        pl.semaphore_signal(barrier, inc=1, device_id={"pix": peer}, device_id_type=MESH)

    a = lax.broadcasted_iota(jnp.int32, (128, 256), 0)
    b = lax.broadcasted_iota(jnp.int32, (128, 256), 1)
    chosen = 16 * ((z + FAR[0] + (a // 2) % 8) % ZN) + 2 * (a // 16) + a % 2
    pick_far = (b == chosen).astype(F32).astype(BF16)
    loads[9].wait()
    tbuf[1] = dot(pick_far, parv[...]).astype(BF16)

    pl.semaphore_wait(barrier, len(peers))
    for k in (4, 12):
        peer = ((z + k) % ZN) * XYN + xy
        pl.semaphore_signal(far_sem, inc=1, device_id={"pix": peer}, device_id_type=MESH)

    def remote(src, dst, send, recv, peer):
        return pltpu.make_async_remote_copy(
            src_ref=src, dst_ref=dst, send_sem=send, recv_sem=recv,
            device_id={"pix": peer}, device_id_type=MESH,
        )

    to_left = remote(fine.at[pl.ds(0, HALO)], halo.at[1], hs_sem.at[0], hr_sem.at[0], left)
    to_right = remote(
        fine.at[pl.ds(rows - HALO, HALO)], halo.at[0], hs_sem.at[1], hr_sem.at[1], right
    )

    own = [
        pltpu.make_async_copy(
            par.at[pl.ds(pl.multiple_of(16 * z, 16), 16)], zbuf.at[0, pl.ds(0, 16)], own_sem.at[0]
        ),
        pltpu.make_async_copy(pslot.at[z // 8], zslot.at[0], own_sem.at[1]),
    ]
    for copy in own:
        copy.start()
    own.append(pltpu.make_async_copy(pslot, xslot.at[0], own_sem.at[2]))
    own[2].start()
    along_z = {}
    for kk, k in enumerate(NEAR):
        if k == 0:
            continue
        there = (z + k) % ZN
        peer = there * XYN + xy
        data = remote(
            par.at[pl.ds(pl.multiple_of(16 * there, 16), 16)],
            zbuf.at[0, pl.ds(16 * kk, 16)],
            zs_sem.at[k], zr_sem.at[k], peer,
        )
        slot = remote(pslot.at[there // 8], zslot.at[kk], zss_sem.at[k], zsr_sem.at[k], peer)
        along_z[k] = (data, slot)
    far_plane = []
    for m in range(1, XYN):
        there = (xy + m) % XYN
        peer = z * XYN + there
        data = remote(
            tbuf.at[1, pl.ds(pl.multiple_of(16 * there, 16), 16)],
            zbuf.at[1, pl.ds(16 * m, 16)],
            ps_sem.at[1, m], pr_sem.at[1, m], peer,
        )
        slot = remote(pslot, xslot.at[m], pss_sem.at[1, m], psr_sem.at[1, m], peer)
        far_plane.append((data, slot))
    for i, k in enumerate((4, 12 + 1, 3, 14, 2, 15, 1)):
        far_plane[i][1].start()
        far_plane[i][0].start()
        along_z[k][1].start()
        along_z[k][0].start()
    loads[4].wait()
    loads[5].wait()
    place = lax.broadcasted_iota(jnp.int32, (8, 128), 0) * 128 + lax.broadcasted_iota(
        jnp.int32, (8, 128), 1
    )
    away = shv[...] - (place + me * rows)
    away = jnp.where(away > total // 2, away - total, away)
    away = jnp.where(away < -(total // 2), away + total, away)
    rel = ((place % WIN) + away + HALO).astype(F32)
    for i in range(8):
        relb[128 * i : 128 * (i + 1), :] = jnp.transpose(
            jnp.broadcast_to(rel[i : i + 1, :], (128, 128))
        )
    gain = fgv[...]
    for i in range(4):
        loads[i].wait()

        def norm_step(s, carry):
            at = pl.multiple_of(WIN * i + 64 * s, 64)
            ext[pl.ds(pl.multiple_of(at + HALO, 64), 64), :] = rms_rows(xv[pl.ds(at, 64), :], gain)
            return carry

        lax.fori_loop(0, WIN // 64, norm_step, 0)
    loads[6].wait()
    wvt[...] = jnp.transpose(wq[:, 2 * features :])

    for data, slot in far_plane:
        slot.wait_recv()
    own[2].wait()
    tables = xslot[...].reshape(16, 128).astype(F32)
    tables = tables.reshape(8, 2, 128)
    tables = jnp.concatenate([tables[:, 0, :], tables[:, 1, :]], axis=1)
    ka = lax.broadcasted_iota(jnp.int32, (8, 256), 0)
    kb = lax.broadcasted_iota(jnp.int32, (8, 256), 1)
    slots = None
    for t in range(2):
        hit = (kb == 16 * ((z + FAR[0] + ka) % ZN) + 2 * xy + t).astype(F32).astype(BF16)
        parts = [jnp.zeros((8, 256), F32)] * 16
        parts[t] = tables
        part = dot(hit, jnp.concatenate(parts, axis=0).astype(BF16), NT)
        slots = part if slots is None else slots + part
    for kk in range(8):
        yslot[kk] = slots[kk : kk + 1, :]
    for data, slot in far_plane:
        data.wait_recv()
    zbuf[1, 0:16, :] = tbuf[1, pl.ds(pl.multiple_of(16 * xy, 16), 16), :]
    a = lax.broadcasted_iota(jnp.int32, (128, 128), 0)
    b = lax.broadcasted_iota(jnp.int32, (128, 128), 1)
    order = (b == (a % 8) * 16 + (a // 16) * 2 + (a // 8) % 2).astype(F32).astype(BF16)
    xbuf[...] = dot(order, zbuf[1]).astype(BF16)
    far_z = []
    for kk, k in enumerate(FAR):
        peer = ((z + k) % ZN) * XYN + xy
        data = remote(
            xbuf.at[pl.ds(16 * kk, 16)], fbuf.at[1, pl.ds(16 * kk, 16)],
            zs_sem.at[k], zr_sem.at[k], peer,
        )
        slot = remote(yslot.at[kk], sslot.at[kk], zss_sem.at[k], zsr_sem.at[k], peer)
        far_z.append((data, slot))
    pl.semaphore_wait(far_sem, 2)
    for i in (3, 4, 2, 5, 1, 6, 0, 7):
        far_z[i][1].start()
    for i in (3, 4, 2, 5, 1, 6, 0, 7):
        far_z[i][0].start()
    to_left.start()
    to_right.start()

    lanes128 = lax.broadcasted_iota(jnp.int32, (1, 128), 1)
    lane_rows = lax.broadcasted_iota(jnp.int32, (WIN, 128), 1).astype(F32)
    head_masks = [(lanes128 // 32 == t).astype(F32).astype(BF16) for t in range(4)]

    def window(i, carry):
        w = (i + 1) % windows
        base = pl.multiple_of(w * WIN, WIN)
        own_rows = ext[pl.ds(pl.multiple_of(base + HALO, HALO), WIN), :]
        qv[pl.ds(base, WIN), :] = dot(own_rows, wq[:, :features]).astype(BF16)
        where = relb[pl.ds(base, WIN), :]
        picks = jnp.concatenate(
            [(where == lane_rows + 128.0 * c).astype(F32).astype(BF16) for c in range(4)], axis=1
        )
        gathered = dot(picks, ext[pl.ds(base, 2 * WIN), :]).astype(BF16)
        kv[...] = dot(gathered, wq[:, features : 2 * features]).astype(BF16)
        vt[...] = dot(wvt[...], gathered, NT).astype(BF16)

        def self_scores(h):
            at = 128 * (h // 4)
            keys = kv[:, at : at + 128] * head_masks[h % 4]
            return dot(keys, qv[pl.ds(base, WIN), at : at + 128], NT)

        def self_values(h, weights):
            ot[32 * h : 32 * h + 32, :] = dot(vt[32 * h : 32 * h + 32, :], weights).astype(BF16)

        staged(HEADS, WIN, self_scores, self_values, sbufs, pbufs)
        out[pl.ds(base, WIN), :features] = jnp.transpose(ot[...])
        return carry

    def near_phase():
        for k in NEAR:
            if k == 0:
                own[1].wait()
            else:
                along_z[k][1].wait_recv()
        slots = [
            remote(
                zslot, fslot.at[m], pss_sem.at[0, m], psr_sem.at[0, m],
                z * XYN + (xy + m) % XYN,
            )
            for m in range(1, XYN)
        ]
        for copy in slots:
            copy.start()
        for k in NEAR:
            if k == 0:
                own[0].wait()
            else:
                along_z[k][0].wait_recv()
        tbuf[0] = dot(order, zbuf[0]).astype(BF16)
        fslot[0] = zslot[...]
        fbuf[0, 0:16, :] = tbuf[0, pl.ds(pl.multiple_of(16 * xy, 16), 16), :]
        data = []
        for m in range(1, XYN):
            there = (xy + m) % XYN
            data.append(
                remote(
                    tbuf.at[0, pl.ds(pl.multiple_of(16 * there, 16), 16)],
                    fbuf.at[0, pl.ds(16 * m, 16)],
                    ps_sem.at[0, m], pr_sem.at[0, m], z * XYN + there,
                )
            )
        for copy in data:
            copy.start()
        return data, slots

    lax.fori_loop(0, 1, window, 0)
    near_data, near_slots = near_phase()
    lax.fori_loop(1, 2, window, 0)

    to_left.wait_recv()
    to_right.wait_recv()
    ext[:HALO, :] = rms_rows(halo[0], gain)
    ext[HALO + rows :, :] = rms_rows(halo[1], gain)
    lax.fori_loop(2, 4, window, 0)

    loads[7].wait()
    loads[8].wait()

    for copy in near_slots:
        copy.wait_recv()
    table = jnp.concatenate([fslot[...].reshape(64, 128).astype(F32), jnp.zeros((64, 128), F32)], axis=0)
    first = 16 * (z % 8) + 2 * xy
    wanted = lax.broadcasted_iota(jnp.int32, (8, 128), 0) + first
    select = (lax.broadcasted_iota(jnp.int32, (8, 128), 1) == wanted).astype(F32).astype(BF16)
    slots = dot(select, table.astype(BF16), NT).astype(BF16)
    same = (b // 16 == a // 8) & (b % 8 == a % 8)
    spread = [
        dot(slots, (same & ((b // 8) % 2 == t)).astype(F32).astype(BF16))[t : t + 1, :]
        for t in range(2)
    ]
    near_position = spread[0] + spread[1]
    for data, slot in far_z:
        slot.wait_recv()
    slots = dot(
        sslot[...].reshape(8, 128).astype(BF16), (a == b % 16).astype(F32).astype(BF16)
    )
    held = lax.broadcasted_iota(jnp.int32, (8, 128), 1) // 16 == lax.broadcasted_iota(
        jnp.int32, (8, 128), 0
    )
    far_position = jnp.sum(jnp.where(held, slots, 0.0), axis=0, keepdims=True)
    position = jnp.concatenate([near_position, far_position], axis=1)
    targets = lax.broadcasted_iota(jnp.int32, (256, 256), 0).astype(F32)
    placing = (targets == position).astype(F32).astype(BF16)
    to_left.wait_send()
    to_right.wait_send()
    for pair in list(along_z.values()) + far_plane + far_z:
        for copy in pair:
            copy.wait_send()
    for copy in near_data + near_slots:
        copy.wait_send()
    for copy in near_data + [data for data, slot in far_z]:
        copy.wait_recv()
    parents = dot(placing, fbuf[...].reshape(256, features)).astype(BF16)
    pnormed = rms_rows(parents, pgv[...])
    kpv[...] = dot(pnormed, wp[...]).astype(BF16)
    groups = HEADS // 4

    def cross_scores(u):
        w, at = u // groups, 128 * (u % groups)
        keys = kpv[PWIN * w : PWIN * (w + 1), at : at + 128]
        stacked = jnp.concatenate([keys * mask for mask in head_masks], axis=0)
        return dot(stacked, qv[WIN * w : WIN * (w + 1), at : at + 128], NT)

    def cross_values(u, weights):
        w, at = u // groups, 128 * (u % groups)
        part = kpv[PWIN * w : PWIN * (w + 1), features + at : features + at + 128]
        stacked = jnp.concatenate([part * mask for mask in head_masks], axis=0)
        cot[w, at : at + 128, :] = dot(stacked, weights, TN).astype(BF16)
        if u % groups == groups - 1:
            here = slice(WIN * w, WIN * (w + 1))
            out[here, features:] = jnp.transpose(cot[w])

    staged(windows * groups, PWIN, cross_scores, cross_values, sbufs, pbufs)


def on_device(
    fine_tokens,
    parent_tokens,
    shift_table,
    parent_slot,
    fine_gain,
    parent_gain,
    w_qkv,
    w_parent,
    w_out,
):
    rows, features = fine_tokens.shape
    dma = pltpu.SemaphoreType.DMA
    vmem = pltpu.VMEM
    joined = pl.pallas_call(
        kernel,
        out_shape=jax.ShapeDtypeStruct((rows, 2 * features), BF16),
        in_specs=[pl.BlockSpec(memory_space=pl.ANY)] * 8,
        out_specs=pl.BlockSpec(memory_space=pltpu.VMEM),
        scratch_shapes=[
            vmem((rows, features), BF16),
            vmem((rows + 2 * HALO, features), BF16),
            vmem((2, HALO, features), BF16),
            vmem((rows, features), BF16),
            vmem((WIN, features), BF16),
            vmem((features, WIN), BF16),
            vmem((features, WIN), BF16),
            vmem((rows, 128), F32),
            vmem((8, 128), jnp.int32),
            vmem((1, features), F32),
            vmem((1, features), F32),
            vmem((features, 3 * features), BF16),
            vmem((features, 2 * features), BF16),
            vmem((features, features), BF16),
            vmem((2, 128, features), BF16),
            vmem((2, 128, features), BF16),
            vmem((2, 128, features), BF16),
            vmem((8, 1, 128), jnp.int32),
            vmem((8, 8, 1, 128), jnp.int32),
            vmem((256, features), BF16),
            vmem((128, features), BF16),
            vmem((8, 2, 1, 128), jnp.int32),
            vmem((8, 1, 128), F32),
            vmem((8, 1, 128), F32),
            vmem((256, 2 * features), BF16),
            vmem((4, features, WIN), BF16),
            *[vmem((WIN, WIN), F32)] * 4,
            *[vmem((WIN, WIN), BF16)] * 4,
            dma((10,)),
            dma((3,)),
            dma((2,)),
            dma((2,)),
            dma((ZN,)),
            dma((ZN,)),
            dma((ZN,)),
            dma((ZN,)),
            dma((2, XYN)),
            dma((2, XYN)),
            dma((2, XYN)),
            dma((2, XYN)),
            pltpu.SemaphoreType.REGULAR,
        ],
        compiler_params=pltpu.CompilerParams(collective_id=0, has_side_effects=True, vmem_limit_bytes=25165824),
    )(
        *[
            pltpu.with_memory_space_constraint(x, pltpu.HBM)
            for x in (
                fine_tokens,
                parent_tokens,
                shift_table.reshape(8, 128),
                parent_slot.reshape(2, 1, 128),
                fine_gain.reshape(1, features),
                parent_gain.reshape(1, features),
                w_qkv,
                w_parent,
            )
        ]
    )
    branch = jnp.dot(joined, w_out, preferred_element_type=F32)
    return (fine_tokens.astype(F32) + branch).astype(BF16)


def solution(mesh):
    return jax.shard_map(
        on_device,
        mesh=mesh,
        in_specs=(
            P(("batch", "pix"), None),
            P(("batch", "pix"), None),
            P("pix"),
            P("pix"),
            P(),
            P(),
            P(),
            P(),
            P(),
        ),
        out_specs=P(("batch", "pix"), None),
        check_vma=False,
    )
```

```python
import functools

import jax
import jax.numpy as jnp
from jax import lax
from jax.experimental import pallas as pl
from jax.experimental.pallas import tpu as pltpu
from jax.sharding import PartitionSpec as P

HEADS = 16
WIN = 256
HALO = 128
PWIN = 64
ZN = 16
XYN = 8
NEAR = (0, 1, 2, 3, 4, 13, 14, 15)
FAR = (5, 6, 7, 8, 9, 10, 11, 12)
MESH = pl.DeviceIdType.MESH
F32 = jnp.float32
BF16 = jnp.bfloat16
SCALE = 1.4426950408889634 / (32.0**0.5)

NN = (((1,), (0,)), ((), ()))
NT = (((1,), (1,)), ((), ()))
TN = (((0,), (0,)), ((), ()))


def dot(a, b, dims=NN):
    return lax.dot_general(a, b, dims, preferred_element_type=F32)


def rms_rows(rows, gain):
    values = rows.astype(F32)
    factor = lax.rsqrt(jnp.mean(values * values, axis=-1, keepdims=True) + 1e-06)
    return (values * factor * gain).astype(BF16)


def softmax_rows(scores):
    powers = jnp.exp2((scores - jnp.max(scores, axis=0, keepdims=True)) * SCALE)
    return (powers * (1.0 / jnp.sum(powers, axis=0, keepdims=True))).astype(BF16)


def staged(units, depth, scores, values, sbufs, pbufs):
    slots = len(sbufs)
    for u in range(-2, units + 2):
        if 0 <= u + 2 < units:
            sbufs[(u + 2) % slots][...] = scores(u + 2)
        if 0 <= u < units:
            for c in range(2):
                cols = slice(128 * c, 128 * (c + 1))
                for first in range(0, WIN, depth):
                    block = slice(first, first + depth)
                    pbufs[u % slots][block, cols] = softmax_rows(sbufs[u % slots][block, cols])
        if 0 <= u - 2 < units:
            values(u - 2, pbufs[(u - 2) % slots][...])


def kernel(
    fine, par, shift, pslot, fgain, pgain, wqkv, wpar, out,
    xv, ext, halo, qv, kv, vt, ot, relb, shv, fgv, pgv,
    wq, wp, wvt, zbuf, tbuf, fbuf, zslot, fslot, parv, xbuf, xslot, yslot, sslot, kpv, cot,
    s0, s1, s2, s3, p0, p1, p2, p3,
    in_sem, own_sem, hs_sem, hr_sem, zs_sem, zr_sem, zss_sem, zsr_sem,
    ps_sem, pr_sem, pss_sem, psr_sem, far_sem,
):
    sbufs, pbufs = (s0, s1, s2, s3), (p0, p1, p2, p3)
    me = lax.axis_index("pix")
    count = ZN * XYN
    z = me // XYN
    xy = me % XYN
    right = (me + 1) % count
    left = (me + count - 1) % count
    rows = xv.shape[0]
    features = xv.shape[1]
    windows = rows // WIN
    total = rows * count

    loads = [
        pltpu.make_async_copy(fine.at[pl.ds(WIN * i, WIN)], xv.at[pl.ds(WIN * i, WIN)], in_sem.at[i])
        for i in range(4)
    ]
    loads.append(pltpu.make_async_copy(fgain, fgv, in_sem.at[4]))
    loads.append(pltpu.make_async_copy(shift, shv, in_sem.at[5]))
    loads.append(pltpu.make_async_copy(wqkv, wq, in_sem.at[6]))
    loads.append(pltpu.make_async_copy(wpar, wp, in_sem.at[7]))
    loads.append(pltpu.make_async_copy(pgain, pgv, in_sem.at[8]))
    loads.append(pltpu.make_async_copy(par, parv, in_sem.at[9]))

    barrier = pltpu.get_barrier_semaphore()
    for i in (9, 0, 4, 5, 1, 2, 3, 6, 7, 8):
        loads[i].start()
    peers = [((z + k) % ZN) * XYN + xy for k in NEAR[1:] + (12,)]
    peers += [z * XYN + (xy + m) % XYN for m in range(1, XYN)]
    peers += [left, right]
    for peer in peers:
        pl.semaphore_signal(barrier, inc=1, device_id={"pix": peer}, device_id_type=MESH)

    a = lax.broadcasted_iota(jnp.int32, (128, 256), 0)
    b = lax.broadcasted_iota(jnp.int32, (128, 256), 1)
    chosen = 16 * ((z + FAR[0] + (a // 2) % 8) % ZN) + 2 * (a // 16) + a % 2
    pick_far = (b == chosen).astype(F32).astype(BF16)
    loads[9].wait()
    tbuf[1] = dot(pick_far, parv[...]).astype(BF16)

    pl.semaphore_wait(barrier, len(peers))
    for k in (4, 12):
        peer = ((z + k) % ZN) * XYN + xy
        pl.semaphore_signal(far_sem, inc=1, device_id={"pix": peer}, device_id_type=MESH)

    def remote(src, dst, send, recv, peer):
        return pltpu.make_async_remote_copy(
            src_ref=src, dst_ref=dst, send_sem=send, recv_sem=recv,
            device_id={"pix": peer}, device_id_type=MESH,
        )

    to_left = remote(fine.at[pl.ds(0, HALO)], halo.at[1], hs_sem.at[0], hr_sem.at[0], left)
    to_right = remote(
        fine.at[pl.ds(rows - HALO, HALO)], halo.at[0], hs_sem.at[1], hr_sem.at[1], right
    )

    own = [
        pltpu.make_async_copy(
            par.at[pl.ds(pl.multiple_of(16 * z, 16), 16)], zbuf.at[0, pl.ds(0, 16)], own_sem.at[0]
        ),
        pltpu.make_async_copy(pslot.at[z // 8], zslot.at[0], own_sem.at[1]),
    ]
    for copy in own:
        copy.start()
    own.append(pltpu.make_async_copy(pslot, xslot.at[0], own_sem.at[2]))
    own[2].start()
    along_z = {}
    for kk, k in enumerate(NEAR):
        if k == 0:
            continue
        there = (z + k) % ZN
        peer = there * XYN + xy
        data = remote(
            par.at[pl.ds(pl.multiple_of(16 * there, 16), 16)],
            zbuf.at[0, pl.ds(16 * kk, 16)],
            zs_sem.at[k], zr_sem.at[k], peer,
        )
        slot = remote(pslot.at[there // 8], zslot.at[kk], zss_sem.at[k], zsr_sem.at[k], peer)
        along_z[k] = (data, slot)
    far_plane = []
    for m in range(1, XYN):
        there = (xy + m) % XYN
        peer = z * XYN + there
        data = remote(
            tbuf.at[1, pl.ds(pl.multiple_of(16 * there, 16), 16)],
            zbuf.at[1, pl.ds(16 * m, 16)],
            ps_sem.at[1, m], pr_sem.at[1, m], peer,
        )
        slot = remote(pslot, xslot.at[m], pss_sem.at[1, m], psr_sem.at[1, m], peer)
        far_plane.append((data, slot))
    for i, k in enumerate((4, 12 + 1, 3, 14, 2, 15, 1)):
        far_plane[i][1].start()
        far_plane[i][0].start()
        along_z[k][1].start()
        along_z[k][0].start()
    loads[4].wait()
    loads[5].wait()
    place = lax.broadcasted_iota(jnp.int32, (8, 128), 0) * 128 + lax.broadcasted_iota(
        jnp.int32, (8, 128), 1
    )
    away = shv[...] - (place + me * rows)
    away = jnp.where(away > total // 2, away - total, away)
    away = jnp.where(away < -(total // 2), away + total, away)
    rel = ((place % WIN) + away + HALO).astype(F32)
    for i in range(8):
        relb[128 * i : 128 * (i + 1), :] = jnp.transpose(
            jnp.broadcast_to(rel[i : i + 1, :], (128, 128))
        )
    gain = fgv[...]
    for i in range(4):
        loads[i].wait()

        def norm_step(s, carry):
            at = pl.multiple_of(WIN * i + 64 * s, 64)
            ext[pl.ds(pl.multiple_of(at + HALO, 64), 64), :] = rms_rows(xv[pl.ds(at, 64), :], gain)
            return carry

        lax.fori_loop(0, WIN // 64, norm_step, 0)
    loads[6].wait()
    wvt[...] = jnp.transpose(wq[:, 2 * features :])

    for data, slot in far_plane:
        slot.wait_recv()
    own[2].wait()
    tables = xslot[...].reshape(16, 128).astype(F32)
    tables = tables.reshape(8, 2, 128)
    tables = jnp.concatenate([tables[:, 0, :], tables[:, 1, :]], axis=1)
    ka = lax.broadcasted_iota(jnp.int32, (8, 256), 0)
    kb = lax.broadcasted_iota(jnp.int32, (8, 256), 1)
    slots = None
    for t in range(2):
        hit = (kb == 16 * ((z + FAR[0] + ka) % ZN) + 2 * xy + t).astype(F32).astype(BF16)
        parts = [jnp.zeros((8, 256), F32)] * 16
        parts[t] = tables
        part = dot(hit, jnp.concatenate(parts, axis=0).astype(BF16), NT)
        slots = part if slots is None else slots + part
    for kk in range(8):
        yslot[kk] = slots[kk : kk + 1, :]
    for data, slot in far_plane:
        data.wait_recv()
    to_left.start()
    to_right.start()
    zbuf[1, 0:16, :] = tbuf[1, pl.ds(pl.multiple_of(16 * xy, 16), 16), :]
    a = lax.broadcasted_iota(jnp.int32, (128, 128), 0)
    b = lax.broadcasted_iota(jnp.int32, (128, 128), 1)
    order = (b == (a % 8) * 16 + (a // 16) * 2 + (a // 8) % 2).astype(F32).astype(BF16)
    xbuf[...] = dot(order, zbuf[1]).astype(BF16)
    far_z = []
    for kk, k in enumerate(FAR):
        peer = ((z + k) % ZN) * XYN + xy
        data = remote(
            xbuf.at[pl.ds(16 * kk, 16)], fbuf.at[1, pl.ds(16 * kk, 16)],
            zs_sem.at[k], zr_sem.at[k], peer,
        )
        slot = remote(yslot.at[kk], sslot.at[kk], zss_sem.at[k], zsr_sem.at[k], peer)
        far_z.append((data, slot))
    pl.semaphore_wait(far_sem, 2)
    for i in (3, 4, 2, 5, 1, 6, 0, 7):
        far_z[i][1].start()
    for i in (3, 4, 2, 5, 1, 6, 0, 7):
        far_z[i][0].start()

    lanes128 = lax.broadcasted_iota(jnp.int32, (1, 128), 1)
    lane_rows = lax.broadcasted_iota(jnp.int32, (WIN, 128), 1).astype(F32)
    head_masks = [(lanes128 // 32 == t).astype(F32).astype(BF16) for t in range(4)]

    def window(i, carry):
        w = (i + 1) % windows
        base = pl.multiple_of(w * WIN, WIN)
        own_rows = ext[pl.ds(pl.multiple_of(base + HALO, HALO), WIN), :]
        qv[pl.ds(base, WIN), :] = dot(own_rows, wq[:, :features]).astype(BF16)
        where = relb[pl.ds(base, WIN), :]
        picks = jnp.concatenate(
            [(where == lane_rows + 128.0 * c).astype(F32).astype(BF16) for c in range(4)], axis=1
        )
        gathered = dot(picks, ext[pl.ds(base, 2 * WIN), :]).astype(BF16)
        kv[...] = dot(gathered, wq[:, features : 2 * features]).astype(BF16)
        vt[...] = dot(wvt[...], gathered, NT).astype(BF16)

        def self_scores(h):
            at = 128 * (h // 4)
            keys = kv[:, at : at + 128] * head_masks[h % 4]
            return dot(keys, qv[pl.ds(base, WIN), at : at + 128], NT)

        def self_values(h, weights):
            ot[32 * h : 32 * h + 32, :] = dot(vt[32 * h : 32 * h + 32, :], weights).astype(BF16)

        staged(HEADS, WIN, self_scores, self_values, sbufs, pbufs)
        out[pl.ds(base, WIN), :features] = jnp.transpose(ot[...])
        return carry

    def near_phase():
        for k in NEAR:
            if k == 0:
                own[1].wait()
            else:
                along_z[k][1].wait_recv()
        slots = [
            remote(
                zslot, fslot.at[m], pss_sem.at[0, m], psr_sem.at[0, m],
                z * XYN + (xy + m) % XYN,
            )
            for m in range(1, XYN)
        ]
        for copy in slots:
            copy.start()
        for k in NEAR:
            if k == 0:
                own[0].wait()
            else:
                along_z[k][0].wait_recv()
        tbuf[0] = dot(order, zbuf[0]).astype(BF16)
        fslot[0] = zslot[...]
        fbuf[0, 0:16, :] = tbuf[0, pl.ds(pl.multiple_of(16 * xy, 16), 16), :]
        data = []
        for m in range(1, XYN):
            there = (xy + m) % XYN
            data.append(
                remote(
                    tbuf.at[0, pl.ds(pl.multiple_of(16 * there, 16), 16)],
                    fbuf.at[0, pl.ds(16 * m, 16)],
                    ps_sem.at[0, m], pr_sem.at[0, m], z * XYN + there,
                )
            )
        for copy in data:
            copy.start()
        return data, slots

    lax.fori_loop(0, 1, window, 0)
    near_data, near_slots = near_phase()
    lax.fori_loop(1, 2, window, 0)

    to_left.wait_recv()
    to_right.wait_recv()
    ext[:HALO, :] = rms_rows(halo[0], gain)
    ext[HALO + rows :, :] = rms_rows(halo[1], gain)
    lax.fori_loop(2, 4, window, 0)

    loads[7].wait()
    loads[8].wait()

    for copy in near_slots:
        copy.wait_recv()
    table = jnp.concatenate([fslot[...].reshape(64, 128).astype(F32), jnp.zeros((64, 128), F32)], axis=0)
    first = 16 * (z % 8) + 2 * xy
    wanted = lax.broadcasted_iota(jnp.int32, (8, 128), 0) + first
    select = (lax.broadcasted_iota(jnp.int32, (8, 128), 1) == wanted).astype(F32).astype(BF16)
    slots = dot(select, table.astype(BF16), NT).astype(BF16)
    same = (b // 16 == a // 8) & (b % 8 == a % 8)
    spread = [
        dot(slots, (same & ((b // 8) % 2 == t)).astype(F32).astype(BF16))[t : t + 1, :]
        for t in range(2)
    ]
    near_position = spread[0] + spread[1]
    for data, slot in far_z:
        slot.wait_recv()
    slots = dot(
        sslot[...].reshape(8, 128).astype(BF16), (a == b % 16).astype(F32).astype(BF16)
    )
    held = lax.broadcasted_iota(jnp.int32, (8, 128), 1) // 16 == lax.broadcasted_iota(
        jnp.int32, (8, 128), 0
    )
    far_position = jnp.sum(jnp.where(held, slots, 0.0), axis=0, keepdims=True)
    position = jnp.concatenate([near_position, far_position], axis=1)
    targets = lax.broadcasted_iota(jnp.int32, (256, 256), 0).astype(F32)
    placing = (targets == position).astype(F32).astype(BF16)
    to_left.wait_send()
    to_right.wait_send()
    for pair in list(along_z.values()) + far_plane + far_z:
        for copy in pair:
            copy.wait_send()
    for copy in near_data + near_slots:
        copy.wait_send()
    for copy in near_data + [data for data, slot in far_z]:
        copy.wait_recv()
    parents = dot(placing, fbuf[...].reshape(256, features)).astype(BF16)
    pnormed = rms_rows(parents, pgv[...])
    kpv[...] = dot(pnormed, wp[...]).astype(BF16)
    groups = HEADS // 4

    def cross_scores(u):
        w, at = u // groups, 128 * (u % groups)
        keys = kpv[PWIN * w : PWIN * (w + 1), at : at + 128]
        stacked = jnp.concatenate([keys * mask for mask in head_masks], axis=0)
        return dot(stacked, qv[WIN * w : WIN * (w + 1), at : at + 128], NT)

    def cross_values(u, weights):
        w, at = u // groups, 128 * (u % groups)
        part = kpv[PWIN * w : PWIN * (w + 1), features + at : features + at + 128]
        stacked = jnp.concatenate([part * mask for mask in head_masks], axis=0)
        cot[w, at : at + 128, :] = dot(stacked, weights, TN).astype(BF16)
        if u % groups == groups - 1:
            here = slice(WIN * w, WIN * (w + 1))
            out[here, features:] = jnp.transpose(cot[w])

    staged(windows * groups, PWIN, cross_scores, cross_values, sbufs, pbufs)


def on_device(
    fine_tokens,
    parent_tokens,
    shift_table,
    parent_slot,
    fine_gain,
    parent_gain,
    w_qkv,
    w_parent,
    w_out,
):
    rows, features = fine_tokens.shape
    dma = pltpu.SemaphoreType.DMA
    vmem = pltpu.VMEM
    joined = pl.pallas_call(
        kernel,
        out_shape=jax.ShapeDtypeStruct((rows, 2 * features), BF16),
        in_specs=[pl.BlockSpec(memory_space=pl.ANY)] * 8,
        out_specs=pl.BlockSpec(memory_space=pltpu.VMEM),
        scratch_shapes=[
            vmem((rows, features), BF16),
            vmem((rows + 2 * HALO, features), BF16),
            vmem((2, HALO, features), BF16),
            vmem((rows, features), BF16),
            vmem((WIN, features), BF16),
            vmem((features, WIN), BF16),
            vmem((features, WIN), BF16),
            vmem((rows, 128), F32),
            vmem((8, 128), jnp.int32),
            vmem((1, features), F32),
            vmem((1, features), F32),
            vmem((features, 3 * features), BF16),
            vmem((features, 2 * features), BF16),
            vmem((features, features), BF16),
            vmem((2, 128, features), BF16),
            vmem((2, 128, features), BF16),
            vmem((2, 128, features), BF16),
            vmem((8, 1, 128), jnp.int32),
            vmem((8, 8, 1, 128), jnp.int32),
            vmem((256, features), BF16),
            vmem((128, features), BF16),
            vmem((8, 2, 1, 128), jnp.int32),
            vmem((8, 1, 128), F32),
            vmem((8, 1, 128), F32),
            vmem((256, 2 * features), BF16),
            vmem((4, features, WIN), BF16),
            *[vmem((WIN, WIN), F32)] * 4,
            *[vmem((WIN, WIN), BF16)] * 4,
            dma((10,)),
            dma((3,)),
            dma((2,)),
            dma((2,)),
            dma((ZN,)),
            dma((ZN,)),
            dma((ZN,)),
            dma((ZN,)),
            dma((2, XYN)),
            dma((2, XYN)),
            dma((2, XYN)),
            dma((2, XYN)),
            pltpu.SemaphoreType.REGULAR,
        ],
        compiler_params=pltpu.CompilerParams(collective_id=0, has_side_effects=True, vmem_limit_bytes=25165824),
    )(
        *[
            pltpu.with_memory_space_constraint(x, pltpu.HBM)
            for x in (
                fine_tokens,
                parent_tokens,
                shift_table.reshape(8, 128),
                parent_slot.reshape(2, 1, 128),
                fine_gain.reshape(1, features),
                parent_gain.reshape(1, features),
                w_qkv,
                w_parent,
            )
        ]
    )
    branch = jnp.dot(joined, w_out, preferred_element_type=F32)
    return (fine_tokens.astype(F32) + branch).astype(BF16)


def solution(mesh):
    return jax.shard_map(
        on_device,
        mesh=mesh,
        in_specs=(
            P(("batch", "pix"), None),
            P(("batch", "pix"), None),
            P("pix"),
            P("pix"),
            P(),
            P(),
            P(),
            P(),
            P(),
        ),
        out_specs=P(("batch", "pix"), None),
        check_vma=False,
    )
```

```python
import functools

import jax
import jax.numpy as jnp
from jax import lax
from jax.experimental import pallas as pl
from jax.experimental.pallas import tpu as pltpu
from jax.sharding import PartitionSpec as P

HEADS = 16
WIN = 256
HALO = 128
PWIN = 64
ZN = 16
XYN = 8
NEAR = (0, 1, 2, 3, 4, 13, 14, 15)
FAR = (5, 6, 7, 8, 9, 10, 11, 12)
MESH = pl.DeviceIdType.MESH
F32 = jnp.float32
BF16 = jnp.bfloat16
SCALE = 1.4426950408889634 / (32.0**0.5)

NN = (((1,), (0,)), ((), ()))
NT = (((1,), (1,)), ((), ()))
TN = (((0,), (0,)), ((), ()))


def dot(a, b, dims=NN):
    return lax.dot_general(a, b, dims, preferred_element_type=F32)


def rms_rows(rows, gain):
    values = rows.astype(F32)
    factor = lax.rsqrt(jnp.mean(values * values, axis=-1, keepdims=True) + 1e-06)
    return (values * factor * gain).astype(BF16)


def softmax_rows(scores):
    powers = jnp.exp2((scores - jnp.max(scores, axis=0, keepdims=True)) * SCALE)
    return (powers * (1.0 / jnp.sum(powers, axis=0, keepdims=True))).astype(BF16)


def staged(units, depth, scores, values, sbufs, pbufs):
    slots = len(sbufs)
    for u in range(-2, units + 2):
        if 0 <= u + 2 < units:
            sbufs[(u + 2) % slots][...] = scores(u + 2)
        if 0 <= u < units:
            for c in range(2):
                cols = slice(128 * c, 128 * (c + 1))
                for first in range(0, WIN, depth):
                    block = slice(first, first + depth)
                    pbufs[u % slots][block, cols] = softmax_rows(sbufs[u % slots][block, cols])
        if 0 <= u - 2 < units:
            values(u - 2, pbufs[(u - 2) % slots][...])


def kernel(
    fine, par, shift, pslot, fgain, pgain, wqkv, wpar, out,
    xv, ext, halo, qv, kv, vt, ot, relb, shv, fgv, pgv,
    wq, wp, wvt, zbuf, tbuf, fbuf, zslot, fslot, parv, xbuf, xslot, yslot, sslot, kpv, cot,
    s0, s1, s2, s3, p0, p1, p2, p3,
    in_sem, own_sem, hs_sem, hr_sem, zs_sem, zr_sem, zss_sem, zsr_sem,
    ps_sem, pr_sem, pss_sem, psr_sem, far_sem,
):
    sbufs, pbufs = (s0, s1, s2, s3), (p0, p1, p2, p3)
    me = lax.axis_index("pix")
    count = ZN * XYN
    z = me // XYN
    xy = me % XYN
    right = (me + 1) % count
    left = (me + count - 1) % count
    rows = xv.shape[0]
    features = xv.shape[1]
    windows = rows // WIN
    total = rows * count

    loads = [
        pltpu.make_async_copy(fine.at[pl.ds(WIN * i, WIN)], xv.at[pl.ds(WIN * i, WIN)], in_sem.at[i])
        for i in range(4)
    ]
    loads.append(pltpu.make_async_copy(fgain, fgv, in_sem.at[4]))
    loads.append(pltpu.make_async_copy(shift, shv, in_sem.at[5]))
    loads.append(pltpu.make_async_copy(wqkv, wq, in_sem.at[6]))
    loads.append(pltpu.make_async_copy(wpar, wp, in_sem.at[7]))
    loads.append(pltpu.make_async_copy(pgain, pgv, in_sem.at[8]))
    loads.append(pltpu.make_async_copy(par, parv, in_sem.at[9]))

    barrier = pltpu.get_barrier_semaphore()
    for i in (9, 0, 4, 5, 1, 2, 3, 6, 7, 8):
        loads[i].start()
    peers = [((z + k) % ZN) * XYN + xy for k in NEAR[1:] + (12,)]
    peers += [z * XYN + (xy + m) % XYN for m in range(1, XYN)]
    peers += [left, right]
    for peer in peers:
        pl.semaphore_signal(barrier, inc=1, device_id={"pix": peer}, device_id_type=MESH)

    a = lax.broadcasted_iota(jnp.int32, (128, 256), 0)
    b = lax.broadcasted_iota(jnp.int32, (128, 256), 1)
    chosen = 16 * ((z + FAR[0] + (a // 2) % 8) % ZN) + 2 * (a // 16) + a % 2
    pick_far = (b == chosen).astype(F32).astype(BF16)
    loads[9].wait()
    tbuf[1] = dot(pick_far, parv[...]).astype(BF16)

    pl.semaphore_wait(barrier, len(peers))
    for k in (4, 12):
        peer = ((z + k) % ZN) * XYN + xy
        pl.semaphore_signal(far_sem, inc=1, device_id={"pix": peer}, device_id_type=MESH)

    def remote(src, dst, send, recv, peer):
        return pltpu.make_async_remote_copy(
            src_ref=src, dst_ref=dst, send_sem=send, recv_sem=recv,
            device_id={"pix": peer}, device_id_type=MESH,
        )

    to_left = remote(fine.at[pl.ds(0, HALO)], halo.at[1], hs_sem.at[0], hr_sem.at[0], left)
    to_right = remote(
        fine.at[pl.ds(rows - HALO, HALO)], halo.at[0], hs_sem.at[1], hr_sem.at[1], right
    )

    own = [
        pltpu.make_async_copy(
            par.at[pl.ds(pl.multiple_of(16 * z, 16), 16)], zbuf.at[0, pl.ds(0, 16)], own_sem.at[0]
        ),
        pltpu.make_async_copy(pslot.at[z // 8], zslot.at[0], own_sem.at[1]),
    ]
    for copy in own:
        copy.start()
    own.append(pltpu.make_async_copy(pslot, xslot.at[0], own_sem.at[2]))
    own[2].start()
    along_z = {}
    for kk, k in enumerate(NEAR):
        if k == 0:
            continue
        there = (z + k) % ZN
        peer = there * XYN + xy
        data = remote(
            par.at[pl.ds(pl.multiple_of(16 * there, 16), 16)],
            zbuf.at[0, pl.ds(16 * kk, 16)],
            zs_sem.at[k], zr_sem.at[k], peer,
        )
        slot = remote(pslot.at[there // 8], zslot.at[kk], zss_sem.at[k], zsr_sem.at[k], peer)
        along_z[k] = (data, slot)
    far_plane = []
    for m in range(1, XYN):
        there = (xy + m) % XYN
        peer = z * XYN + there
        data = remote(
            tbuf.at[1, pl.ds(pl.multiple_of(16 * there, 16), 16)],
            zbuf.at[1, pl.ds(16 * m, 16)],
            ps_sem.at[1, m], pr_sem.at[1, m], peer,
        )
        slot = remote(pslot, xslot.at[m], pss_sem.at[1, m], psr_sem.at[1, m], peer)
        far_plane.append((data, slot))
    for i, k in enumerate((4, 12 + 1, 3, 14, 2, 15, 1)):
        far_plane[i][1].start()
        far_plane[i][0].start()
        along_z[k][1].start()
        along_z[k][0].start()

    @pl.when(xy == 0)
    def _():
        to_left.start()

    @pl.when(xy == XYN - 1)
    def _():
        to_right.start()

    loads[4].wait()
    loads[5].wait()
    place = lax.broadcasted_iota(jnp.int32, (8, 128), 0) * 128 + lax.broadcasted_iota(
        jnp.int32, (8, 128), 1
    )
    away = shv[...] - (place + me * rows)
    away = jnp.where(away > total // 2, away - total, away)
    away = jnp.where(away < -(total // 2), away + total, away)
    rel = ((place % WIN) + away + HALO).astype(F32)
    for i in range(8):
        relb[128 * i : 128 * (i + 1), :] = jnp.transpose(
            jnp.broadcast_to(rel[i : i + 1, :], (128, 128))
        )
    gain = fgv[...]
    for i in range(4):
        loads[i].wait()

        def norm_step(s, carry):
            at = pl.multiple_of(WIN * i + 64 * s, 64)
            ext[pl.ds(pl.multiple_of(at + HALO, 64), 64), :] = rms_rows(xv[pl.ds(at, 64), :], gain)
            return carry

        lax.fori_loop(0, WIN // 64, norm_step, 0)
    loads[6].wait()
    wvt[...] = jnp.transpose(wq[:, 2 * features :])

    for data, slot in far_plane:
        slot.wait_recv()
    own[2].wait()
    tables = xslot[...].reshape(16, 128).astype(F32)
    tables = tables.reshape(8, 2, 128)
    tables = jnp.concatenate([tables[:, 0, :], tables[:, 1, :]], axis=1)
    ka = lax.broadcasted_iota(jnp.int32, (8, 256), 0)
    kb = lax.broadcasted_iota(jnp.int32, (8, 256), 1)
    slots = None
    for t in range(2):
        hit = (kb == 16 * ((z + FAR[0] + ka) % ZN) + 2 * xy + t).astype(F32).astype(BF16)
        parts = [jnp.zeros((8, 256), F32)] * 16
        parts[t] = tables
        part = dot(hit, jnp.concatenate(parts, axis=0).astype(BF16), NT)
        slots = part if slots is None else slots + part
    for kk in range(8):
        yslot[kk] = slots[kk : kk + 1, :]
    for data, slot in far_plane:
        data.wait_recv()

    @pl.when(xy != 0)
    def _():
        to_left.start()

    @pl.when(xy != XYN - 1)
    def _():
        to_right.start()

    zbuf[1, 0:16, :] = tbuf[1, pl.ds(pl.multiple_of(16 * xy, 16), 16), :]
    a = lax.broadcasted_iota(jnp.int32, (128, 128), 0)
    b = lax.broadcasted_iota(jnp.int32, (128, 128), 1)
    order = (b == (a % 8) * 16 + (a // 16) * 2 + (a // 8) % 2).astype(F32).astype(BF16)
    xbuf[...] = dot(order, zbuf[1]).astype(BF16)
    far_z = []
    for kk, k in enumerate(FAR):
        peer = ((z + k) % ZN) * XYN + xy
        data = remote(
            xbuf.at[pl.ds(16 * kk, 16)], fbuf.at[1, pl.ds(16 * kk, 16)],
            zs_sem.at[k], zr_sem.at[k], peer,
        )
        slot = remote(yslot.at[kk], sslot.at[kk], zss_sem.at[k], zsr_sem.at[k], peer)
        far_z.append((data, slot))
    pl.semaphore_wait(far_sem, 2)
    for i in (3, 4, 2, 5, 1, 6, 0, 7):
        far_z[i][1].start()
    for i in (3, 4, 2, 5, 1, 6, 0, 7):
        far_z[i][0].start()

    lanes128 = lax.broadcasted_iota(jnp.int32, (1, 128), 1)
    lane_rows = lax.broadcasted_iota(jnp.int32, (WIN, 128), 1).astype(F32)
    head_masks = [(lanes128 // 32 == t).astype(F32).astype(BF16) for t in range(4)]

    def window(i, carry):
        w = (i + 1) % windows
        base = pl.multiple_of(w * WIN, WIN)
        own_rows = ext[pl.ds(pl.multiple_of(base + HALO, HALO), WIN), :]
        qv[pl.ds(base, WIN), :] = dot(own_rows, wq[:, :features]).astype(BF16)
        where = relb[pl.ds(base, WIN), :]
        picks = jnp.concatenate(
            [(where == lane_rows + 128.0 * c).astype(F32).astype(BF16) for c in range(4)], axis=1
        )
        gathered = dot(picks, ext[pl.ds(base, 2 * WIN), :]).astype(BF16)
        kv[...] = dot(gathered, wq[:, features : 2 * features]).astype(BF16)
        vt[...] = dot(wvt[...], gathered, NT).astype(BF16)

        def self_scores(h):
            at = 128 * (h // 4)
            keys = kv[:, at : at + 128] * head_masks[h % 4]
            return dot(keys, qv[pl.ds(base, WIN), at : at + 128], NT)

        def self_values(h, weights):
            ot[32 * h : 32 * h + 32, :] = dot(vt[32 * h : 32 * h + 32, :], weights).astype(BF16)

        staged(HEADS, WIN, self_scores, self_values, sbufs, pbufs)
        out[pl.ds(base, WIN), :features] = jnp.transpose(ot[...])
        return carry

    def near_phase():
        for k in NEAR:
            if k == 0:
                own[1].wait()
            else:
                along_z[k][1].wait_recv()
        slots = [
            remote(
                zslot, fslot.at[m], pss_sem.at[0, m], psr_sem.at[0, m],
                z * XYN + (xy + m) % XYN,
            )
            for m in range(1, XYN)
        ]
        for copy in slots:
            copy.start()
        for k in NEAR:
            if k == 0:
                own[0].wait()
            else:
                along_z[k][0].wait_recv()
        tbuf[0] = dot(order, zbuf[0]).astype(BF16)
        fslot[0] = zslot[...]
        fbuf[0, 0:16, :] = tbuf[0, pl.ds(pl.multiple_of(16 * xy, 16), 16), :]
        data = []
        for m in range(1, XYN):
            there = (xy + m) % XYN
            data.append(
                remote(
                    tbuf.at[0, pl.ds(pl.multiple_of(16 * there, 16), 16)],
                    fbuf.at[0, pl.ds(16 * m, 16)],
                    ps_sem.at[0, m], pr_sem.at[0, m], z * XYN + there,
                )
            )
        for copy in data:
            copy.start()
        return data, slots

    lax.fori_loop(0, 1, window, 0)
    near_data, near_slots = near_phase()
    lax.fori_loop(1, 2, window, 0)

    to_left.wait_recv()
    to_right.wait_recv()
    ext[:HALO, :] = rms_rows(halo[0], gain)
    ext[HALO + rows :, :] = rms_rows(halo[1], gain)
    lax.fori_loop(2, 4, window, 0)

    loads[7].wait()
    loads[8].wait()

    for copy in near_slots:
        copy.wait_recv()
    table = jnp.concatenate([fslot[...].reshape(64, 128).astype(F32), jnp.zeros((64, 128), F32)], axis=0)
    first = 16 * (z % 8) + 2 * xy
    wanted = lax.broadcasted_iota(jnp.int32, (8, 128), 0) + first
    select = (lax.broadcasted_iota(jnp.int32, (8, 128), 1) == wanted).astype(F32).astype(BF16)
    slots = dot(select, table.astype(BF16), NT).astype(BF16)
    same = (b // 16 == a // 8) & (b % 8 == a % 8)
    spread = [
        dot(slots, (same & ((b // 8) % 2 == t)).astype(F32).astype(BF16))[t : t + 1, :]
        for t in range(2)
    ]
    near_position = spread[0] + spread[1]
    for data, slot in far_z:
        slot.wait_recv()
    slots = dot(
        sslot[...].reshape(8, 128).astype(BF16), (a == b % 16).astype(F32).astype(BF16)
    )
    held = lax.broadcasted_iota(jnp.int32, (8, 128), 1) // 16 == lax.broadcasted_iota(
        jnp.int32, (8, 128), 0
    )
    far_position = jnp.sum(jnp.where(held, slots, 0.0), axis=0, keepdims=True)
    position = jnp.concatenate([near_position, far_position], axis=1)
    targets = lax.broadcasted_iota(jnp.int32, (256, 256), 0).astype(F32)
    placing = (targets == position).astype(F32).astype(BF16)
    to_left.wait_send()
    to_right.wait_send()
    for pair in list(along_z.values()) + far_plane + far_z:
        for copy in pair:
            copy.wait_send()
    for copy in near_data + near_slots:
        copy.wait_send()
    for copy in near_data + [data for data, slot in far_z]:
        copy.wait_recv()
    parents = dot(placing, fbuf[...].reshape(256, features)).astype(BF16)
    pnormed = rms_rows(parents, pgv[...])
    kpv[...] = dot(pnormed, wp[...]).astype(BF16)
    groups = HEADS // 4

    def cross_scores(u):
        w, at = u // groups, 128 * (u % groups)
        keys = kpv[PWIN * w : PWIN * (w + 1), at : at + 128]
        stacked = jnp.concatenate([keys * mask for mask in head_masks], axis=0)
        return dot(stacked, qv[WIN * w : WIN * (w + 1), at : at + 128], NT)

    def cross_values(u, weights):
        w, at = u // groups, 128 * (u % groups)
        part = kpv[PWIN * w : PWIN * (w + 1), features + at : features + at + 128]
        stacked = jnp.concatenate([part * mask for mask in head_masks], axis=0)
        cot[w, at : at + 128, :] = dot(stacked, weights, TN).astype(BF16)
        if u % groups == groups - 1:
            here = slice(WIN * w, WIN * (w + 1))
            out[here, features:] = jnp.transpose(cot[w])

    staged(windows * groups, PWIN, cross_scores, cross_values, sbufs, pbufs)


def on_device(
    fine_tokens,
    parent_tokens,
    shift_table,
    parent_slot,
    fine_gain,
    parent_gain,
    w_qkv,
    w_parent,
    w_out,
):
    rows, features = fine_tokens.shape
    dma = pltpu.SemaphoreType.DMA
    vmem = pltpu.VMEM
    joined = pl.pallas_call(
        kernel,
        out_shape=jax.ShapeDtypeStruct((rows, 2 * features), BF16),
        in_specs=[pl.BlockSpec(memory_space=pl.ANY)] * 8,
        out_specs=pl.BlockSpec(memory_space=pltpu.VMEM),
        scratch_shapes=[
            vmem((rows, features), BF16),
            vmem((rows + 2 * HALO, features), BF16),
            vmem((2, HALO, features), BF16),
            vmem((rows, features), BF16),
            vmem((WIN, features), BF16),
            vmem((features, WIN), BF16),
            vmem((features, WIN), BF16),
            vmem((rows, 128), F32),
            vmem((8, 128), jnp.int32),
            vmem((1, features), F32),
            vmem((1, features), F32),
            vmem((features, 3 * features), BF16),
            vmem((features, 2 * features), BF16),
            vmem((features, features), BF16),
            vmem((2, 128, features), BF16),
            vmem((2, 128, features), BF16),
            vmem((2, 128, features), BF16),
            vmem((8, 1, 128), jnp.int32),
            vmem((8, 8, 1, 128), jnp.int32),
            vmem((256, features), BF16),
            vmem((128, features), BF16),
            vmem((8, 2, 1, 128), jnp.int32),
            vmem((8, 1, 128), F32),
            vmem((8, 1, 128), F32),
            vmem((256, 2 * features), BF16),
            vmem((4, features, WIN), BF16),
            *[vmem((WIN, WIN), F32)] * 4,
            *[vmem((WIN, WIN), BF16)] * 4,
            dma((10,)),
            dma((3,)),
            dma((2,)),
            dma((2,)),
            dma((ZN,)),
            dma((ZN,)),
            dma((ZN,)),
            dma((ZN,)),
            dma((2, XYN)),
            dma((2, XYN)),
            dma((2, XYN)),
            dma((2, XYN)),
            pltpu.SemaphoreType.REGULAR,
        ],
        compiler_params=pltpu.CompilerParams(collective_id=0, has_side_effects=True, vmem_limit_bytes=25165824),
    )(
        *[
            pltpu.with_memory_space_constraint(x, pltpu.HBM)
            for x in (
                fine_tokens,
                parent_tokens,
                shift_table.reshape(8, 128),
                parent_slot.reshape(2, 1, 128),
                fine_gain.reshape(1, features),
                parent_gain.reshape(1, features),
                w_qkv,
                w_parent,
            )
        ]
    )
    branch = jnp.dot(joined, w_out, preferred_element_type=F32)
    return (fine_tokens.astype(F32) + branch).astype(BF16)


def solution(mesh):
    return jax.shard_map(
        on_device,
        mesh=mesh,
        in_specs=(
            P(("batch", "pix"), None),
            P(("batch", "pix"), None),
            P("pix"),
            P("pix"),
            P(),
            P(),
            P(),
            P(),
            P(),
        ),
        out_specs=P(("batch", "pix"), None),
        check_vma=False,
    )
```

```python
import functools

import jax
import jax.numpy as jnp
from jax import lax
from jax.experimental import pallas as pl
from jax.experimental.pallas import tpu as pltpu
from jax.sharding import PartitionSpec as P

HEADS = 16
WIN = 256
HALO = 128
PWIN = 64
ZN = 16
XYN = 8
NEAR = (0, 1, 2, 3, 4, 13, 14, 15)
FAR = (5, 6, 7, 8, 9, 10, 11, 12)
MESH = pl.DeviceIdType.MESH
F32 = jnp.float32
BF16 = jnp.bfloat16
SCALE = 1.4426950408889634 / (32.0**0.5)

NN = (((1,), (0,)), ((), ()))
NT = (((1,), (1,)), ((), ()))
TN = (((0,), (0,)), ((), ()))


def dot(a, b, dims=NN):
    return lax.dot_general(a, b, dims, preferred_element_type=F32)


def rms_rows(rows, gain):
    values = rows.astype(F32)
    factor = lax.rsqrt(jnp.mean(values * values, axis=-1, keepdims=True) + 1e-06)
    return (values * factor * gain).astype(BF16)


def softmax_rows(scores):
    powers = jnp.exp2((scores - jnp.max(scores, axis=0, keepdims=True)) * SCALE)
    return (powers * (1.0 / jnp.sum(powers, axis=0, keepdims=True))).astype(BF16)


def staged(units, depth, scores, values, sbufs, pbufs):
    slots = len(sbufs)
    for u in range(-2, units + 2):
        if 0 <= u + 2 < units:
            sbufs[(u + 2) % slots][...] = scores(u + 2)
        if 0 <= u < units:
            for c in range(2):
                cols = slice(128 * c, 128 * (c + 1))
                for first in range(0, WIN, depth):
                    block = slice(first, first + depth)
                    pbufs[u % slots][block, cols] = softmax_rows(sbufs[u % slots][block, cols])
        if 0 <= u - 2 < units:
            values(u - 2, pbufs[(u - 2) % slots][...])


def kernel(
    fine, par, shift, pslot, fgain, pgain, wqkv, wpar, out,
    xv, ext, halo, qv, kv, vt, ot, relb, shv, fgv, pgv,
    wq, wp, wvt, zbuf, tbuf, fbuf, zslot, fslot, parv, xbuf, xslot, yslot, sslot, kpv, cot,
    s0, s1, s2, s3, p0, p1, p2, p3,
    in_sem, own_sem, hs_sem, hr_sem, zs_sem, zr_sem, zss_sem, zsr_sem,
    ps_sem, pr_sem, pss_sem, psr_sem, far_sem,
):
    sbufs, pbufs = (s0, s1, s2, s3), (p0, p1, p2, p3)
    me = lax.axis_index("pix")
    count = ZN * XYN
    z = me // XYN
    xy = me % XYN
    right = (me + 1) % count
    left = (me + count - 1) % count
    rows = xv.shape[0]
    features = xv.shape[1]
    windows = rows // WIN
    total = rows * count

    loads = [
        pltpu.make_async_copy(fine.at[pl.ds(WIN * i, WIN)], xv.at[pl.ds(WIN * i, WIN)], in_sem.at[i])
        for i in range(4)
    ]
    loads.append(pltpu.make_async_copy(fgain, fgv, in_sem.at[4]))
    loads.append(pltpu.make_async_copy(shift, shv, in_sem.at[5]))
    loads.append(pltpu.make_async_copy(wqkv, wq, in_sem.at[6]))
    loads.append(pltpu.make_async_copy(wpar, wp, in_sem.at[7]))
    loads.append(pltpu.make_async_copy(pgain, pgv, in_sem.at[8]))
    loads.append(pltpu.make_async_copy(par, parv, in_sem.at[9]))

    barrier = pltpu.get_barrier_semaphore()
    for i in (9, 0, 4, 5, 1, 2, 3, 6, 7, 8):
        loads[i].start()
    peers = [((z + k) % ZN) * XYN + xy for k in NEAR[1:] + (12,)]
    peers += [z * XYN + (xy + m) % XYN for m in range(1, XYN)]
    peers += [left, right]
    for peer in peers:
        pl.semaphore_signal(barrier, inc=1, device_id={"pix": peer}, device_id_type=MESH)

    pl.semaphore_wait(barrier, len(peers))
    for k in (4, 12):
        peer = ((z + k) % ZN) * XYN + xy
        pl.semaphore_signal(far_sem, inc=1, device_id={"pix": peer}, device_id_type=MESH)

    def remote(src, dst, send, recv, peer):
        return pltpu.make_async_remote_copy(
            src_ref=src, dst_ref=dst, send_sem=send, recv_sem=recv,
            device_id={"pix": peer}, device_id_type=MESH,
        )

    to_left = remote(fine.at[pl.ds(0, HALO)], halo.at[1], hs_sem.at[0], hr_sem.at[0], left)
    to_right = remote(
        fine.at[pl.ds(rows - HALO, HALO)], halo.at[0], hs_sem.at[1], hr_sem.at[1], right
    )

    own = [
        pltpu.make_async_copy(
            par.at[pl.ds(pl.multiple_of(16 * z, 16), 16)], zbuf.at[0, pl.ds(0, 16)], own_sem.at[0]
        ),
        pltpu.make_async_copy(pslot.at[z // 8], zslot.at[0], own_sem.at[1]),
    ]
    for copy in own:
        copy.start()
    own.append(pltpu.make_async_copy(pslot, xslot.at[0], own_sem.at[2]))
    own[2].start()
    along_z = {}
    for kk, k in enumerate(NEAR):
        if k == 0:
            continue
        there = (z + k) % ZN
        peer = there * XYN + xy
        data = remote(
            par.at[pl.ds(pl.multiple_of(16 * there, 16), 16)],
            zbuf.at[0, pl.ds(16 * kk, 16)],
            zs_sem.at[k], zr_sem.at[k], peer,
        )
        slot = remote(pslot.at[there // 8], zslot.at[kk], zss_sem.at[k], zsr_sem.at[k], peer)
        along_z[k] = (data, slot)
    far_plane = []
    for m in range(1, XYN):
        there = (xy + m) % XYN
        peer = z * XYN + there
        data = remote(
            tbuf.at[1, pl.ds(pl.multiple_of(16 * there, 16), 16)],
            zbuf.at[1, pl.ds(16 * m, 16)],
            ps_sem.at[1, m], pr_sem.at[1, m], peer,
        )
        slot = remote(pslot, xslot.at[m], pss_sem.at[1, m], psr_sem.at[1, m], peer)
        far_plane.append((data, slot))
    for i, k in enumerate((4, 13, 3, 14, 2, 15, 1)):
        far_plane[i][1].start()
        along_z[k][1].start()
        along_z[k][0].start()

    @pl.when(xy == 0)
    def _():
        to_left.start()

    @pl.when(xy == XYN - 1)
    def _():
        to_right.start()

    a = lax.broadcasted_iota(jnp.int32, (128, 256), 0)
    b = lax.broadcasted_iota(jnp.int32, (128, 256), 1)
    chosen = 16 * ((z + FAR[0] + (a // 2) % 8) % ZN) + 2 * (a // 16) + a % 2
    pick_far = (b == chosen).astype(F32).astype(BF16)
    loads[9].wait()
    tbuf[1] = dot(pick_far, parv[...]).astype(BF16)
    zbuf[1, 0:16, :] = tbuf[1, pl.ds(pl.multiple_of(16 * xy, 16), 16), :]
    for data, slot in far_plane:
        data.start()

    loads[4].wait()
    loads[5].wait()
    place = lax.broadcasted_iota(jnp.int32, (8, 128), 0) * 128 + lax.broadcasted_iota(
        jnp.int32, (8, 128), 1
    )
    away = shv[...] - (place + me * rows)
    away = jnp.where(away > total // 2, away - total, away)
    away = jnp.where(away < -(total // 2), away + total, away)
    rel = ((place % WIN) + away + HALO).astype(F32)
    for i in range(8):
        relb[128 * i : 128 * (i + 1), :] = jnp.transpose(
            jnp.broadcast_to(rel[i : i + 1, :], (128, 128))
        )
    gain = fgv[...]
    for i in range(4):
        loads[i].wait()

        def norm_step(s, carry):
            at = pl.multiple_of(WIN * i + 64 * s, 64)
            ext[pl.ds(pl.multiple_of(at + HALO, 64), 64), :] = rms_rows(xv[pl.ds(at, 64), :], gain)
            return carry

        lax.fori_loop(0, WIN // 64, norm_step, 0)
    loads[6].wait()
    wvt[...] = jnp.transpose(wq[:, 2 * features :])

    for data, slot in far_plane:
        slot.wait_recv()
    own[2].wait()
    tables = xslot[...].reshape(16, 128).astype(F32)
    tables = tables.reshape(8, 2, 128)
    tables = jnp.concatenate([tables[:, 0, :], tables[:, 1, :]], axis=1)
    ka = lax.broadcasted_iota(jnp.int32, (8, 256), 0)
    kb = lax.broadcasted_iota(jnp.int32, (8, 256), 1)
    slots = None
    for t in range(2):
        hit = (kb == 16 * ((z + FAR[0] + ka) % ZN) + 2 * xy + t).astype(F32).astype(BF16)
        parts = [jnp.zeros((8, 256), F32)] * 16
        parts[t] = tables
        part = dot(hit, jnp.concatenate(parts, axis=0).astype(BF16), NT)
        slots = part if slots is None else slots + part
    for kk in range(8):
        yslot[kk] = slots[kk : kk + 1, :]
    for data, slot in far_plane:
        data.wait_recv()

    @pl.when(xy != 0)
    def _():
        to_left.start()

    @pl.when(xy != XYN - 1)
    def _():
        to_right.start()

    a = lax.broadcasted_iota(jnp.int32, (128, 128), 0)
    b = lax.broadcasted_iota(jnp.int32, (128, 128), 1)
    order = (b == (a % 8) * 16 + (a // 16) * 2 + (a // 8) % 2).astype(F32).astype(BF16)
    xbuf[...] = dot(order, zbuf[1]).astype(BF16)
    far_z = []
    for kk, k in enumerate(FAR):
        peer = ((z + k) % ZN) * XYN + xy
        data = remote(
            xbuf.at[pl.ds(16 * kk, 16)], fbuf.at[1, pl.ds(16 * kk, 16)],
            zs_sem.at[k], zr_sem.at[k], peer,
        )
        slot = remote(yslot.at[kk], sslot.at[kk], zss_sem.at[k], zsr_sem.at[k], peer)
        far_z.append((data, slot))
    pl.semaphore_wait(far_sem, 2)
    for i in (3, 4, 2, 5, 1, 6, 0, 7):
        far_z[i][1].start()
    for i in (3, 4, 2, 5, 1, 6, 0, 7):
        far_z[i][0].start()

    lanes128 = lax.broadcasted_iota(jnp.int32, (1, 128), 1)
    lane_rows = lax.broadcasted_iota(jnp.int32, (WIN, 128), 1).astype(F32)
    head_masks = [(lanes128 // 32 == t).astype(F32).astype(BF16) for t in range(4)]

    def window(i, carry):
        w = (i + 1) % windows
        base = pl.multiple_of(w * WIN, WIN)
        own_rows = ext[pl.ds(pl.multiple_of(base + HALO, HALO), WIN), :]
        qv[pl.ds(base, WIN), :] = dot(own_rows, wq[:, :features]).astype(BF16)
        where = relb[pl.ds(base, WIN), :]
        picks = jnp.concatenate(
            [(where == lane_rows + 128.0 * c).astype(F32).astype(BF16) for c in range(4)], axis=1
        )
        gathered = dot(picks, ext[pl.ds(base, 2 * WIN), :]).astype(BF16)
        kv[...] = dot(gathered, wq[:, features : 2 * features]).astype(BF16)
        vt[...] = dot(wvt[...], gathered, NT).astype(BF16)

        def self_scores(h):
            at = 128 * (h // 4)
            keys = kv[:, at : at + 128] * head_masks[h % 4]
            return dot(keys, qv[pl.ds(base, WIN), at : at + 128], NT)

        def self_values(h, weights):
            ot[32 * h : 32 * h + 32, :] = dot(vt[32 * h : 32 * h + 32, :], weights).astype(BF16)

        staged(HEADS, WIN, self_scores, self_values, sbufs, pbufs)
        out[pl.ds(base, WIN), :features] = jnp.transpose(ot[...])
        return carry

    def near_phase():
        for k in NEAR:
            if k == 0:
                own[1].wait()
            else:
                along_z[k][1].wait_recv()
        slots = [
            remote(
                zslot, fslot.at[m], pss_sem.at[0, m], psr_sem.at[0, m],
                z * XYN + (xy + m) % XYN,
            )
            for m in range(1, XYN)
        ]
        for copy in slots:
            copy.start()
        for k in NEAR:
            if k == 0:
                own[0].wait()
            else:
                along_z[k][0].wait_recv()
        tbuf[0] = dot(order, zbuf[0]).astype(BF16)
        fslot[0] = zslot[...]
        fbuf[0, 0:16, :] = tbuf[0, pl.ds(pl.multiple_of(16 * xy, 16), 16), :]
        data = []
        for m in range(1, XYN):
            there = (xy + m) % XYN
            data.append(
                remote(
                    tbuf.at[0, pl.ds(pl.multiple_of(16 * there, 16), 16)],
                    fbuf.at[0, pl.ds(16 * m, 16)],
                    ps_sem.at[0, m], pr_sem.at[0, m], z * XYN + there,
                )
            )
        for copy in data:
            copy.start()
        return data, slots

    lax.fori_loop(0, 1, window, 0)
    near_data, near_slots = near_phase()
    lax.fori_loop(1, 2, window, 0)

    to_left.wait_recv()
    to_right.wait_recv()
    ext[:HALO, :] = rms_rows(halo[0], gain)
    ext[HALO + rows :, :] = rms_rows(halo[1], gain)
    lax.fori_loop(2, 4, window, 0)

    loads[7].wait()
    loads[8].wait()

    for copy in near_slots:
        copy.wait_recv()
    table = jnp.concatenate([fslot[...].reshape(64, 128).astype(F32), jnp.zeros((64, 128), F32)], axis=0)
    first = 16 * (z % 8) + 2 * xy
    wanted = lax.broadcasted_iota(jnp.int32, (8, 128), 0) + first
    select = (lax.broadcasted_iota(jnp.int32, (8, 128), 1) == wanted).astype(F32).astype(BF16)
    slots = dot(select, table.astype(BF16), NT).astype(BF16)
    same = (b // 16 == a // 8) & (b % 8 == a % 8)
    spread = [
        dot(slots, (same & ((b // 8) % 2 == t)).astype(F32).astype(BF16))[t : t + 1, :]
        for t in range(2)
    ]
    near_position = spread[0] + spread[1]
    for data, slot in far_z:
        slot.wait_recv()
    slots = dot(
        sslot[...].reshape(8, 128).astype(BF16), (a == b % 16).astype(F32).astype(BF16)
    )
    held = lax.broadcasted_iota(jnp.int32, (8, 128), 1) // 16 == lax.broadcasted_iota(
        jnp.int32, (8, 128), 0
    )
    far_position = jnp.sum(jnp.where(held, slots, 0.0), axis=0, keepdims=True)
    position = jnp.concatenate([near_position, far_position], axis=1)
    targets = lax.broadcasted_iota(jnp.int32, (256, 256), 0).astype(F32)
    placing = (targets == position).astype(F32).astype(BF16)
    to_left.wait_send()
    to_right.wait_send()
    for pair in list(along_z.values()) + far_plane + far_z:
        for copy in pair:
            copy.wait_send()
    for copy in near_data + near_slots:
        copy.wait_send()
    for copy in near_data + [data for data, slot in far_z]:
        copy.wait_recv()
    parents = dot(placing, fbuf[...].reshape(256, features)).astype(BF16)
    pnormed = rms_rows(parents, pgv[...])
    kpv[...] = dot(pnormed, wp[...]).astype(BF16)
    groups = HEADS // 4

    def cross_scores(u):
        w, at = u // groups, 128 * (u % groups)
        keys = kpv[PWIN * w : PWIN * (w + 1), at : at + 128]
        stacked = jnp.concatenate([keys * mask for mask in head_masks], axis=0)
        return dot(stacked, qv[WIN * w : WIN * (w + 1), at : at + 128], NT)

    def cross_values(u, weights):
        w, at = u // groups, 128 * (u % groups)
        part = kpv[PWIN * w : PWIN * (w + 1), features + at : features + at + 128]
        stacked = jnp.concatenate([part * mask for mask in head_masks], axis=0)
        cot[w, at : at + 128, :] = dot(stacked, weights, TN).astype(BF16)
        if u % groups == groups - 1:
            here = slice(WIN * w, WIN * (w + 1))
            out[here, features:] = jnp.transpose(cot[w])

    staged(windows * groups, PWIN, cross_scores, cross_values, sbufs, pbufs)


def on_device(
    fine_tokens,
    parent_tokens,
    shift_table,
    parent_slot,
    fine_gain,
    parent_gain,
    w_qkv,
    w_parent,
    w_out,
):
    rows, features = fine_tokens.shape
    dma = pltpu.SemaphoreType.DMA
    vmem = pltpu.VMEM
    joined = pl.pallas_call(
        kernel,
        out_shape=jax.ShapeDtypeStruct((rows, 2 * features), BF16),
        in_specs=[pl.BlockSpec(memory_space=pl.ANY)] * 8,
        out_specs=pl.BlockSpec(memory_space=pltpu.VMEM),
        scratch_shapes=[
            vmem((rows, features), BF16),
            vmem((rows + 2 * HALO, features), BF16),
            vmem((2, HALO, features), BF16),
            vmem((rows, features), BF16),
            vmem((WIN, features), BF16),
            vmem((features, WIN), BF16),
            vmem((features, WIN), BF16),
            vmem((rows, 128), F32),
            vmem((8, 128), jnp.int32),
            vmem((1, features), F32),
            vmem((1, features), F32),
            vmem((features, 3 * features), BF16),
            vmem((features, 2 * features), BF16),
            vmem((features, features), BF16),
            vmem((2, 128, features), BF16),
            vmem((2, 128, features), BF16),
            vmem((2, 128, features), BF16),
            vmem((8, 1, 128), jnp.int32),
            vmem((8, 8, 1, 128), jnp.int32),
            vmem((256, features), BF16),
            vmem((128, features), BF16),
            vmem((8, 2, 1, 128), jnp.int32),
            vmem((8, 1, 128), F32),
            vmem((8, 1, 128), F32),
            vmem((256, 2 * features), BF16),
            vmem((4, features, WIN), BF16),
            *[vmem((WIN, WIN), F32)] * 4,
            *[vmem((WIN, WIN), BF16)] * 4,
            dma((10,)),
            dma((3,)),
            dma((2,)),
            dma((2,)),
            dma((ZN,)),
            dma((ZN,)),
            dma((ZN,)),
            dma((ZN,)),
            dma((2, XYN)),
            dma((2, XYN)),
            dma((2, XYN)),
            dma((2, XYN)),
            pltpu.SemaphoreType.REGULAR,
        ],
        compiler_params=pltpu.CompilerParams(collective_id=0, has_side_effects=True, vmem_limit_bytes=25165824),
    )(
        *[
            pltpu.with_memory_space_constraint(x, pltpu.HBM)
            for x in (
                fine_tokens,
                parent_tokens,
                shift_table.reshape(8, 128),
                parent_slot.reshape(2, 1, 128),
                fine_gain.reshape(1, features),
                parent_gain.reshape(1, features),
                w_qkv,
                w_parent,
            )
        ]
    )
    branch = jnp.dot(joined, w_out, preferred_element_type=F32)
    return (fine_tokens.astype(F32) + branch).astype(BF16)


def solution(mesh):
    return jax.shard_map(
        on_device,
        mesh=mesh,
        in_specs=(
            P(("batch", "pix"), None),
            P(("batch", "pix"), None),
            P("pix"),
            P("pix"),
            P(),
            P(),
            P(),
            P(),
            P(),
        ),
        out_specs=P(("batch", "pix"), None),
        check_vma=False,
    )
```

```python
import functools

import jax
import jax.numpy as jnp
from jax import lax
from jax.experimental import pallas as pl
from jax.experimental.pallas import tpu as pltpu
from jax.sharding import PartitionSpec as P

HEADS = 16
WIN = 256
HALO = 128
PWIN = 64
ZN = 16
XYN = 8
NEAR = (0, 1, 2, 3, 4, 13, 14, 15)
FAR = (5, 6, 7, 8, 9, 10, 11, 12)
MESH = pl.DeviceIdType.MESH
F32 = jnp.float32
BF16 = jnp.bfloat16
SCALE = 1.4426950408889634 / (32.0**0.5)

NN = (((1,), (0,)), ((), ()))
NT = (((1,), (1,)), ((), ()))
TN = (((0,), (0,)), ((), ()))


def dot(a, b, dims=NN):
    return lax.dot_general(a, b, dims, preferred_element_type=F32)


def rms_rows(rows, gain):
    values = rows.astype(F32)
    factor = lax.rsqrt(jnp.mean(values * values, axis=-1, keepdims=True) + 1e-06)
    return (values * factor * gain).astype(BF16)


def softmax_rows(scores):
    powers = jnp.exp2((scores - jnp.max(scores, axis=0, keepdims=True)) * SCALE)
    return (powers * (1.0 / jnp.sum(powers, axis=0, keepdims=True))).astype(BF16)


def staged(units, depth, scores, values, sbufs, pbufs):
    slots = len(sbufs)
    for u in range(-2, units + 2):
        if 0 <= u + 2 < units:
            sbufs[(u + 2) % slots][...] = scores(u + 2)
        if 0 <= u < units:
            for c in range(2):
                cols = slice(128 * c, 128 * (c + 1))
                for first in range(0, WIN, depth):
                    block = slice(first, first + depth)
                    pbufs[u % slots][block, cols] = softmax_rows(sbufs[u % slots][block, cols])
        if 0 <= u - 2 < units:
            values(u - 2, pbufs[(u - 2) % slots][...])


def kernel(
    fine, par, shift, pslot, fgain, pgain, wqkv, wpar, out,
    xv, ext, halo, qv, kv, vt, ot, relb, shv, fgv, pgv,
    wq, wp, wvt, zbuf, tbuf, fbuf, zslot, fslot, parv, xbuf, xslot, yslot, sslot, kpv,
    s0, s1, s2, s3, p0, p1, p2, p3,
    in_sem, own_sem, hs_sem, hr_sem, zs_sem, zr_sem, zss_sem, zsr_sem,
    ps_sem, pr_sem, pss_sem, psr_sem, far_sem,
):
    sbufs, pbufs = (s0, s1, s2, s3), (p0, p1, p2, p3)
    me = lax.axis_index("pix")
    count = ZN * XYN
    z = me // XYN
    xy = me % XYN
    right = (me + 1) % count
    left = (me + count - 1) % count
    rows = xv.shape[0]
    features = xv.shape[1]
    windows = rows // WIN
    total = rows * count

    loads = [
        pltpu.make_async_copy(fine.at[pl.ds(WIN * i, WIN)], xv.at[pl.ds(WIN * i, WIN)], in_sem.at[i])
        for i in range(4)
    ]
    loads.append(pltpu.make_async_copy(fgain, fgv, in_sem.at[4]))
    loads.append(pltpu.make_async_copy(shift, shv, in_sem.at[5]))
    loads.append(pltpu.make_async_copy(wqkv, wq, in_sem.at[6]))
    loads.append(pltpu.make_async_copy(wpar, wp, in_sem.at[7]))
    loads.append(pltpu.make_async_copy(pgain, pgv, in_sem.at[8]))
    loads.append(pltpu.make_async_copy(par, parv, in_sem.at[9]))

    barrier = pltpu.get_barrier_semaphore()
    for i in (9, 0, 4, 5, 1, 2, 3, 6, 7, 8):
        loads[i].start()
    peers = [((z + k) % ZN) * XYN + xy for k in NEAR[1:] + (12,)]
    peers += [z * XYN + (xy + m) % XYN for m in range(1, XYN)]
    peers += [left, right]
    for peer in peers:
        pl.semaphore_signal(barrier, inc=1, device_id={"pix": peer}, device_id_type=MESH)

    pl.semaphore_wait(barrier, len(peers))
    for k in (4, 12):
        peer = ((z + k) % ZN) * XYN + xy
        pl.semaphore_signal(far_sem, inc=1, device_id={"pix": peer}, device_id_type=MESH)

    def remote(src, dst, send, recv, peer):
        return pltpu.make_async_remote_copy(
            src_ref=src, dst_ref=dst, send_sem=send, recv_sem=recv,
            device_id={"pix": peer}, device_id_type=MESH,
        )

    to_left = remote(fine.at[pl.ds(0, HALO)], halo.at[1], hs_sem.at[0], hr_sem.at[0], left)
    to_right = remote(
        fine.at[pl.ds(rows - HALO, HALO)], halo.at[0], hs_sem.at[1], hr_sem.at[1], right
    )

    own = [
        pltpu.make_async_copy(
            par.at[pl.ds(pl.multiple_of(16 * z, 16), 16)], zbuf.at[0, pl.ds(0, 16)], own_sem.at[0]
        ),
        pltpu.make_async_copy(pslot.at[z // 8], zslot.at[0], own_sem.at[1]),
    ]
    for copy in own:
        copy.start()
    own.append(pltpu.make_async_copy(pslot, xslot.at[0], own_sem.at[2]))
    own[2].start()
    along_z = {}
    for kk, k in enumerate(NEAR):
        if k == 0:
            continue
        there = (z + k) % ZN
        peer = there * XYN + xy
        data = remote(
            par.at[pl.ds(pl.multiple_of(16 * there, 16), 16)],
            zbuf.at[0, pl.ds(16 * kk, 16)],
            zs_sem.at[k], zr_sem.at[k], peer,
        )
        slot = remote(pslot.at[there // 8], zslot.at[kk], zss_sem.at[k], zsr_sem.at[k], peer)
        along_z[k] = (data, slot)
    far_plane = []
    for m in range(1, XYN):
        there = (xy + m) % XYN
        peer = z * XYN + there
        data = remote(
            tbuf.at[1, pl.ds(pl.multiple_of(16 * there, 16), 16)],
            zbuf.at[1, pl.ds(16 * m, 16)],
            ps_sem.at[1, m], pr_sem.at[1, m], peer,
        )
        slot = remote(pslot, xslot.at[m], pss_sem.at[1, m], psr_sem.at[1, m], peer)
        far_plane.append((data, slot))
    for i, k in enumerate((4, 13, 3, 14, 2, 15, 1)):
        far_plane[i][1].start()
        along_z[k][1].start()
        along_z[k][0].start()

    @pl.when(xy == 0)
    def _():
        to_left.start()

    @pl.when(xy == XYN - 1)
    def _():
        to_right.start()

    a = lax.broadcasted_iota(jnp.int32, (128, 256), 0)
    b = lax.broadcasted_iota(jnp.int32, (128, 256), 1)
    chosen = 16 * ((z + FAR[0] + (a // 2) % 8) % ZN) + 2 * (a // 16) + a % 2
    pick_far = (b == chosen).astype(F32).astype(BF16)
    loads[9].wait()
    tbuf[1] = dot(pick_far, parv[...]).astype(BF16)
    zbuf[1, 0:16, :] = tbuf[1, pl.ds(pl.multiple_of(16 * xy, 16), 16), :]
    for data, slot in far_plane:
        data.start()

    loads[4].wait()
    loads[5].wait()
    place = lax.broadcasted_iota(jnp.int32, (8, 128), 0) * 128 + lax.broadcasted_iota(
        jnp.int32, (8, 128), 1
    )
    away = shv[...] - (place + me * rows)
    away = jnp.where(away > total // 2, away - total, away)
    away = jnp.where(away < -(total // 2), away + total, away)
    rel = ((place % WIN) + away + HALO).astype(F32)
    for i in range(8):
        relb[128 * i : 128 * (i + 1), :] = jnp.transpose(
            jnp.broadcast_to(rel[i : i + 1, :], (128, 128))
        )
    gain = fgv[...]
    for i in range(4):
        loads[i].wait()

        def norm_step(s, carry):
            at = pl.multiple_of(WIN * i + 64 * s, 64)
            ext[pl.ds(pl.multiple_of(at + HALO, 64), 64), :] = rms_rows(xv[pl.ds(at, 64), :], gain)
            return carry

        lax.fori_loop(0, WIN // 64, norm_step, 0)
    loads[6].wait()
    wvt[...] = jnp.transpose(wq[:, 2 * features :])

    for data, slot in far_plane:
        slot.wait_recv()
    own[2].wait()
    tables = xslot[...].reshape(16, 128).astype(F32)
    tables = tables.reshape(8, 2, 128)
    tables = jnp.concatenate([tables[:, 0, :], tables[:, 1, :]], axis=1)
    ka = lax.broadcasted_iota(jnp.int32, (8, 256), 0)
    kb = lax.broadcasted_iota(jnp.int32, (8, 256), 1)
    slots = None
    for t in range(2):
        hit = (kb == 16 * ((z + FAR[0] + ka) % ZN) + 2 * xy + t).astype(F32).astype(BF16)
        parts = [jnp.zeros((8, 256), F32)] * 16
        parts[t] = tables
        part = dot(hit, jnp.concatenate(parts, axis=0).astype(BF16), NT)
        slots = part if slots is None else slots + part
    for kk in range(8):
        yslot[kk] = slots[kk : kk + 1, :]
    for data, slot in far_plane:
        data.wait_recv()

    @pl.when(xy != 0)
    def _():
        to_left.start()

    @pl.when(xy != XYN - 1)
    def _():
        to_right.start()

    a = lax.broadcasted_iota(jnp.int32, (128, 128), 0)
    b = lax.broadcasted_iota(jnp.int32, (128, 128), 1)
    order = (b == (a % 8) * 16 + (a // 16) * 2 + (a // 8) % 2).astype(F32).astype(BF16)
    xbuf[...] = dot(order, zbuf[1]).astype(BF16)
    far_z = []
    for kk, k in enumerate(FAR):
        peer = ((z + k) % ZN) * XYN + xy
        data = remote(
            xbuf.at[pl.ds(16 * kk, 16)], fbuf.at[1, pl.ds(16 * kk, 16)],
            zs_sem.at[k], zr_sem.at[k], peer,
        )
        slot = remote(yslot.at[kk], sslot.at[kk], zss_sem.at[k], zsr_sem.at[k], peer)
        far_z.append((data, slot))
    pl.semaphore_wait(far_sem, 2)
    for i in (3, 4, 2, 5, 1, 6, 0, 7):
        far_z[i][1].start()
    for i in (3, 4, 2, 5, 1, 6, 0, 7):
        far_z[i][0].start()

    lanes128 = lax.broadcasted_iota(jnp.int32, (1, 128), 1)
    lane_rows = lax.broadcasted_iota(jnp.int32, (WIN, 128), 1).astype(F32)
    head_masks = [(lanes128 // 32 == t).astype(F32).astype(BF16) for t in range(4)]

    def window(i, carry):
        w = (i + 1) % windows
        base = pl.multiple_of(w * WIN, WIN)
        own_rows = ext[pl.ds(pl.multiple_of(base + HALO, HALO), WIN), :]
        qv[pl.ds(base, WIN), :] = dot(own_rows, wq[:, :features]).astype(BF16)
        where = relb[pl.ds(base, WIN), :]
        picks = jnp.concatenate(
            [(where == lane_rows + 128.0 * c).astype(F32).astype(BF16) for c in range(4)], axis=1
        )
        gathered = dot(picks, ext[pl.ds(base, 2 * WIN), :]).astype(BF16)
        kv[...] = dot(gathered, wq[:, features : 2 * features]).astype(BF16)
        vt[...] = dot(wvt[...], gathered, NT).astype(BF16)

        def self_scores(h):
            at = 128 * (h // 4)
            keys = kv[:, at : at + 128] * head_masks[h % 4]
            return dot(keys, qv[pl.ds(base, WIN), at : at + 128], NT)

        def self_values(h, weights):
            ot[32 * h : 32 * h + 32, :] = dot(vt[32 * h : 32 * h + 32, :], weights).astype(BF16)

        staged(HEADS, WIN, self_scores, self_values, sbufs, pbufs)
        out[pl.ds(base, WIN), :features] = jnp.transpose(ot[...])
        return carry

    def near_phase():
        for k in NEAR:
            if k == 0:
                own[1].wait()
            else:
                along_z[k][1].wait_recv()
        slots = [
            remote(
                zslot, fslot.at[m], pss_sem.at[0, m], psr_sem.at[0, m],
                z * XYN + (xy + m) % XYN,
            )
            for m in range(1, XYN)
        ]
        for copy in slots:
            copy.start()
        for k in NEAR:
            if k == 0:
                own[0].wait()
            else:
                along_z[k][0].wait_recv()
        tbuf[0] = dot(order, zbuf[0]).astype(BF16)
        fslot[0] = zslot[...]
        fbuf[0, 0:16, :] = tbuf[0, pl.ds(pl.multiple_of(16 * xy, 16), 16), :]
        data = []
        for m in range(1, XYN):
            there = (xy + m) % XYN
            data.append(
                remote(
                    tbuf.at[0, pl.ds(pl.multiple_of(16 * there, 16), 16)],
                    fbuf.at[0, pl.ds(16 * m, 16)],
                    ps_sem.at[0, m], pr_sem.at[0, m], z * XYN + there,
                )
            )
        for copy in data:
            copy.start()
        return data, slots

    lax.fori_loop(0, 1, window, 0)
    near_data, near_slots = near_phase()
    lax.fori_loop(1, 2, window, 0)

    to_left.wait_recv()
    to_right.wait_recv()
    ext[:HALO, :] = rms_rows(halo[0], gain)
    ext[HALO + rows :, :] = rms_rows(halo[1], gain)
    lax.fori_loop(2, 4, window, 0)

    loads[7].wait()
    loads[8].wait()

    for copy in near_slots:
        copy.wait_recv()
    table = jnp.concatenate([fslot[...].reshape(64, 128).astype(F32), jnp.zeros((64, 128), F32)], axis=0)
    first = 16 * (z % 8) + 2 * xy
    wanted = lax.broadcasted_iota(jnp.int32, (8, 128), 0) + first
    select = (lax.broadcasted_iota(jnp.int32, (8, 128), 1) == wanted).astype(F32).astype(BF16)
    slots = dot(select, table.astype(BF16), NT).astype(BF16)
    same = (b // 16 == a // 8) & (b % 8 == a % 8)
    spread = [
        dot(slots, (same & ((b // 8) % 2 == t)).astype(F32).astype(BF16))[t : t + 1, :]
        for t in range(2)
    ]
    near_position = spread[0] + spread[1]
    for data, slot in far_z:
        slot.wait_recv()
    slots = dot(
        sslot[...].reshape(8, 128).astype(BF16), (a == b % 16).astype(F32).astype(BF16)
    )
    held = lax.broadcasted_iota(jnp.int32, (8, 128), 1) // 16 == lax.broadcasted_iota(
        jnp.int32, (8, 128), 0
    )
    far_position = jnp.sum(jnp.where(held, slots, 0.0), axis=0, keepdims=True)
    position = jnp.concatenate([near_position, far_position], axis=1)
    targets = lax.broadcasted_iota(jnp.int32, (256, 256), 0).astype(F32)
    placing = (targets == position).astype(F32).astype(BF16)
    to_left.wait_send()
    to_right.wait_send()
    for pair in list(along_z.values()) + far_plane + far_z:
        for copy in pair:
            copy.wait_send()
    for copy in near_data + near_slots:
        copy.wait_send()
    for copy in near_data + [data for data, slot in far_z]:
        copy.wait_recv()
    parents = dot(placing, fbuf[...].reshape(256, features)).astype(BF16)
    pnormed = rms_rows(parents, pgv[...])
    kpv[...] = dot(pnormed, wp[...]).astype(BF16)
    groups = HEADS // 4

    def cross_scores(u):
        w, at = u // groups, 128 * (u % groups)
        keys = kpv[PWIN * w : PWIN * (w + 1), at : at + 128]
        stacked = jnp.concatenate([keys * mask for mask in head_masks], axis=0)
        return dot(stacked, qv[WIN * w : WIN * (w + 1), at : at + 128], NT)

    def cross_values(u, weights):
        w, at = u // groups, 128 * (u % groups)
        part = kpv[PWIN * w : PWIN * (w + 1), features + at : features + at + 128]
        stacked = jnp.concatenate([part * mask for mask in head_masks], axis=0)
        here = slice(WIN * w, WIN * (w + 1))
        result = dot(stacked, weights, TN).astype(BF16)
        out[here, features + at : features + at + 128] = jnp.transpose(result)

    staged(windows * groups, PWIN, cross_scores, cross_values, sbufs, pbufs)


def on_device(
    fine_tokens,
    parent_tokens,
    shift_table,
    parent_slot,
    fine_gain,
    parent_gain,
    w_qkv,
    w_parent,
    w_out,
):
    rows, features = fine_tokens.shape
    dma = pltpu.SemaphoreType.DMA
    vmem = pltpu.VMEM
    joined = pl.pallas_call(
        kernel,
        out_shape=jax.ShapeDtypeStruct((rows, 2 * features), BF16),
        in_specs=[pl.BlockSpec(memory_space=pl.ANY)] * 8,
        out_specs=pl.BlockSpec(memory_space=pltpu.VMEM),
        scratch_shapes=[
            vmem((rows, features), BF16),
            vmem((rows + 2 * HALO, features), BF16),
            vmem((2, HALO, features), BF16),
            vmem((rows, features), BF16),
            vmem((WIN, features), BF16),
            vmem((features, WIN), BF16),
            vmem((features, WIN), BF16),
            vmem((rows, 128), F32),
            vmem((8, 128), jnp.int32),
            vmem((1, features), F32),
            vmem((1, features), F32),
            vmem((features, 3 * features), BF16),
            vmem((features, 2 * features), BF16),
            vmem((features, features), BF16),
            vmem((2, 128, features), BF16),
            vmem((2, 128, features), BF16),
            vmem((2, 128, features), BF16),
            vmem((8, 1, 128), jnp.int32),
            vmem((8, 8, 1, 128), jnp.int32),
            vmem((256, features), BF16),
            vmem((128, features), BF16),
            vmem((8, 2, 1, 128), jnp.int32),
            vmem((8, 1, 128), F32),
            vmem((8, 1, 128), F32),
            vmem((256, 2 * features), BF16),
            *[vmem((WIN, WIN), F32)] * 4,
            *[vmem((WIN, WIN), BF16)] * 4,
            dma((10,)),
            dma((3,)),
            dma((2,)),
            dma((2,)),
            dma((ZN,)),
            dma((ZN,)),
            dma((ZN,)),
            dma((ZN,)),
            dma((2, XYN)),
            dma((2, XYN)),
            dma((2, XYN)),
            dma((2, XYN)),
            pltpu.SemaphoreType.REGULAR,
        ],
        compiler_params=pltpu.CompilerParams(collective_id=0, has_side_effects=True, vmem_limit_bytes=25165824),
    )(
        *[
            pltpu.with_memory_space_constraint(x, pltpu.HBM)
            for x in (
                fine_tokens,
                parent_tokens,
                shift_table.reshape(8, 128),
                parent_slot.reshape(2, 1, 128),
                fine_gain.reshape(1, features),
                parent_gain.reshape(1, features),
                w_qkv,
                w_parent,
            )
        ]
    )
    branch = jnp.dot(joined, w_out, preferred_element_type=F32)
    return (fine_tokens.astype(F32) + branch).astype(BF16)


def solution(mesh):
    return jax.shard_map(
        on_device,
        mesh=mesh,
        in_specs=(
            P(("batch", "pix"), None),
            P(("batch", "pix"), None),
            P("pix"),
            P("pix"),
            P(),
            P(),
            P(),
            P(),
            P(),
        ),
        out_specs=P(("batch", "pix"), None),
        check_vma=False,
    )
```
